128 devices in a mesh: gx: 4 (over y), gy: 4 (over x), gz: 8 (over z, core).
Axes of the slice: x: 4, y: 4, z: 4, core: 2. Of those that a mesh axis runs over, the one named last changes fastest.
Arguments:
- residual_in: float32 [2, 4, 64, 64, 1024], P(None, None, 'gx', 'gy', 'gz'), may hold values from -15 to 15
- reaction: float32 [4, 64, 64, 1024], P(None, 'gx', 'gy', 'gz'), may hold values from 0.5 to 2
- transport: float32 [4, 64, 64, 1024], P(None, 'gx', 'gy', 'gz'), may hold values from 0.2 to 1
- congestion: float32 [4, 64, 64, 1024], P(None, 'gx', 'gy', 'gz'), may hold values from 0.5 to 1.5
Outputs:
- newton_update: float32 [2, 4, 64, 64, 1024], P(None, None, 'gx', 'gy', 'gz')
The draws below stay inside these ranges and needn't reach their ends.
All inputs are finite; a program needn't handle non-finite values.
Results may differ from the reference program's by a relative error of at most 0.0003.
Values sent between devices are 32-bit elements; how exact they have to be, the bound alone decides.
No kernel may reach another device: no remote copies, remote signals or barrier semaphores. Data moves between devices by JAX's collectives and lax.ppermute only.
A program may use at most 128 MiB of HBM per device.

```python
import jax
import jax.numpy as jnp

LEVELS = 4
ITERS = 8
NX = 64
NY = 64
NZ = 1024


def level_of(own_key, shape, cuts, low, top_value):
    factor_of = 1.0
    for dim, blocks in cuts:
        draws = jax.random.uniform(jax.random.fold_in(jax.random.fold_in(own_key, 6), dim), (blocks,), jnp.float32, low / len(cuts), top_value / len(cuts))
        factor_of = factor_of * jnp.repeat(jnp.exp(draws), shape[dim] // blocks).reshape((-1,) + (1,) * (len(shape) - 1 - dim))
    return factor_of


def normal_values(rng, extent, scale, bound, pieces=(), held_as=jnp.bfloat16):
    drawn = jax.random.normal(rng, extent, jnp.float32) * scale
    if len(pieces) > 0:
        drawn = level_of(rng, extent, pieces, -0.22, 0.18) * drawn
    return jnp.clip(drawn, min=-bound, max=bound).astype(held_as)


def setup_inputs(seed: int = 0) -> dict:
    seeds = jax.random.split(jax.random.key(seed), 5)
    return {
        "residual_in": normal_values(seeds[0], (2, LEVELS, NX, NY, NZ), 3.0, 15.0, ((2, 4), (3, 4), (4, 8)), jnp.float32),
        "reaction": jnp.clip(0.5 + 1.5 * jax.random.uniform(seeds[1], (LEVELS, NX, NY, NZ), jnp.float32) ** level_of(seeds[1], (LEVELS, NX, NY, NZ), ((1, 4), (2, 4), (3, 8)), -0.2, 0.2), 0.5, 2.0),
        "transport": jnp.clip(0.2 + 0.8 * jax.random.uniform(seeds[2], (LEVELS, NX, NY, NZ), jnp.float32) ** level_of(seeds[2], (LEVELS, NX, NY, NZ), ((1, 4), (2, 4), (3, 8)), -0.2, 0.2), 0.2, 1.0),
        "congestion": jnp.clip(0.5 + 1.0 * jax.random.uniform(seeds[3], (LEVELS, NX, NY, NZ), jnp.float32) ** level_of(seeds[3], (LEVELS, NX, NY, NZ), ((1, 4), (2, 4), (3, 8)), -0.2, 0.2), 0.5, 1.5),
    }


time_rate = 1.0

def minus_laplace(field):
    padded = jnp.pad(field, ((0, 0), (0, 0), (1, 1), (1, 1), (1, 1)))
    center = padded[:, :, 1:-1, 1:-1, 1:-1]
    beside = padded[:, :, 2:, 1:-1, 1:-1] + padded[:, :, :-2, 1:-1, 1:-1]
    beside = beside + padded[:, :, 1:-1, 2:, 1:-1] + padded[:, :, 1:-1, :-2, 1:-1]
    beside = beside + padded[:, :, 1:-1, 1:-1, 2:] + padded[:, :, 1:-1, 1:-1, :-2]
    return 6.0 * center - beside

def jacobian(vector, lapped, reaction, transport, congestion):
    value_part, density_part = (vector[0], vector[1])
    later = jnp.concatenate([value_part[1:], jnp.zeros_like(value_part[:1])], 0)
    earlier = jnp.concatenate([jnp.zeros_like(density_part[:1]), density_part[:-1]], 0)
    first = time_rate * (value_part - later) + lapped[0] + reaction * value_part - congestion * density_part
    second = time_rate * (density_part - earlier) + lapped[1] + reaction * density_part - transport * lapped[0]
    return jnp.stack([first, second], 0)

def precondition(vector, reaction, transport):
    levels = vector.shape[1]
    diag = time_rate + 6.0 + reaction
    value_levels = [None] * levels
    carry = jnp.zeros_like(vector[0, 0])
    for level in range(levels - 1, -1, -1):
        carry = (vector[0, level] + time_rate * carry) / diag[level]
        value_levels[level] = carry
    density_levels = []
    carry = jnp.zeros_like(vector[1, 0])
    for level in range(levels):
        carry = (vector[1, level] + time_rate * carry + 6.0 * transport[level] * value_levels[level]) / diag[level]
        density_levels.append(carry)
    return jnp.stack([jnp.stack(value_levels, 0), jnp.stack(density_levels, 0)], 0)

def least_squares(columns, beta, steps):
    rotations = []
    target = [beta] + [jnp.float32(0.0)] * steps
    upper = []
    for column_index in range(steps):
        column = list(columns[column_index])
        for place, (cosine, sine) in enumerate(rotations):
            upper_entry = cosine * column[place] + sine * column[place + 1]
            lower_entry = -sine * column[place] + cosine * column[place + 1]
            column[place], column[place + 1] = (upper_entry, lower_entry)
        radius = jnp.sqrt(column[column_index] ** 2 + column[column_index + 1] ** 2)
        cosine = column[column_index] / radius
        sine = column[column_index + 1] / radius
        column[column_index] = radius
        rotations.append((cosine, sine))
        target[column_index], target[column_index + 1] = (cosine * target[column_index], -sine * target[column_index])
        upper.append(column[:column_index + 1])
    solved = [None] * steps
    for row_index in range(steps - 1, -1, -1):
        accum = target[row_index]
        for later_index in range(row_index + 1, steps):
            accum = accum - upper[later_index][row_index] * solved[later_index]
        solved[row_index] = accum / upper[row_index][row_index]
    return solved

def reference(residual_in, reaction, transport, congestion):
    beta = jnp.sqrt(jnp.sum(residual_in * residual_in))
    basis = [residual_in / beta]
    columns = []
    for column_index in range(ITERS):
        search = precondition(basis[column_index], reaction, transport)
        image = jacobian(search, minus_laplace(search), reaction, transport, congestion)
        coeffs = [jnp.sum(vector * image) for vector in basis]
        for coeff, vector in zip(coeffs, basis):
            image = image - coeff * vector
        height = jnp.sqrt(jnp.sum(image * image))
        basis.append(image / height)
        columns.append(coeffs + [height])
    solved = least_squares(columns, beta, ITERS)
    update = jnp.zeros_like(residual_in)
    for column_index in range(ITERS):
        update = update + solved[column_index] * precondition(basis[column_index], reaction, transport)
    return update
```

```python
import functools

import jax
import jax.numpy as jnp
from jax import lax
from jax.experimental import pallas as pl
from jax.experimental.pallas import tpu as pltpu
from jax.sharding import Mesh
from jax.sharding import PartitionSpec as P

ITERS = 8
LEVELS = 4
DEPTH = 4
N = 16
E = N + 2 * DEPTH
LANES = 128
PAD = 8
VECTORS = ITERS + 1
PAIRS = [(i, j) for i in range(VECTORS) for j in range(i, VECTORS)]
ROWS = 48
GZ = ("gz_0", "gz_1")
SHIFT = (0.68, -0.68, 0.0, -0.392, 0.448, -0.57, 0.592, 0.208)
SPREAD = 0.45
F32 = jnp.float32


def vmem(shape):
    return pltpu.VMEM(shape, F32)


def resident(array):
    return pltpu.with_memory_space_constraint(array, pltpu.VMEM)


def call(kernel, outs, *args, scratch=(), smem=0, cost=1000000):
    whole = pl.BlockSpec(memory_space=pltpu.VMEM)
    in_specs = [pl.BlockSpec(memory_space=pltpu.SMEM)] * smem + [whole] * (len(args) - smem)
    return pl.pallas_call(
        kernel,
        out_shape=outs,
        in_specs=in_specs,
        out_specs=[whole] * len(outs),
        scratch_shapes=list(scratch),
        compiler_params=pltpu.CompilerParams(vmem_limit_bytes=LIMIT),
        cost_estimate=pl.CostEstimate(flops=cost, bytes_accessed=cost, transcendentals=0),
    )(*args)


LIMIT = 24 * 1024 * 1024
SLAB = {
    (-1, 0): (slice(0, DEPTH), slice(0, N)),
    (1, 0): (slice(N - DEPTH, N), slice(0, N)),
    (0, -1): (slice(0, N), slice(0, DEPTH)),
    (0, 1): (slice(0, N), slice(N - DEPTH, N)),
    (-1, -1): (slice(0, DEPTH), slice(0, DEPTH)),
    (1, 1): (slice(N - DEPTH, N), slice(N - DEPTH, N)),
    (-1, 1): (slice(0, DEPTH), slice(N - DEPTH, N)),
    (1, -1): (slice(N - DEPTH, N), slice(0, DEPTH)),
}
WAYS = list(SLAB)


def landing(way):
    low = lambda d: DEPTH if d == 0 else (0 if d > 0 else DEPTH + N)
    size = lambda d: N if d == 0 else DEPTH
    return tuple(slice(low(d), low(d) + size(d)) for d in way)


def slab_shape(fields, way):
    return (fields,) + tuple(N if d == 0 else DEPTH for d in way) + (LANES,)


def pack_kernel(res, rea, tra, con, *outs):
    for out, way in zip(outs, WAYS):
        xs, ys = SLAB[way]
        for source, base, count in ((res, 0, 8), (rea, 8, 4), (tra, 12, 4), (con, 16, 4)):
            @pl.loop(0, count)
            def _(f):
                out[base + f] = source[f, xs, ys, :]


def slab_kernel(core, *outs):
    for out, way in zip(outs, WAYS):
        xs, ys = SLAB[way]

        @pl.loop(0, 8)
        def _(f):
            out[f] = core[f, xs, ys, :]


def widen_kernel(sources, *refs):
    cores, slabs = refs[:sources], refs[sources : sources + 8]
    wide, low, high = refs[sources + 8 :]
    base = 0
    for core in cores:
        count = core.shape[0]

        @pl.loop(0, count)
        def _(f):
            wide[base + f, DEPTH : DEPTH + N, DEPTH : DEPTH + N, :] = core[f]

        base = base + count

    slot = lax.broadcasted_iota(jnp.int32, (E, LANES), 1) // DEPTH

    @pl.loop(0, wide.shape[0])
    def _(f):
        for slab, way in zip(slabs, WAYS):
            xs, ys = landing(way)
            wide[f, xs, ys, :] = slab[f]
        lo = jnp.zeros((E, LANES), F32)
        hi = jnp.zeros((E, LANES), F32)
        for x in range(E):
            rolled = pltpu.roll(wide[f, x], DEPTH * x, 1) if x else wide[f, x]
            lo = jnp.where(slot == x, rolled, lo)
            hi = jnp.where(slot == (x - 1) % (LANES // DEPTH), rolled, hi)
        low[f] = lo
        high[f] = hi


def spread_ghosts(zr, zl, slot):
    even = slot % 2 == 0
    return jnp.where(even, zr, zl), jnp.where(even, zl, zr)


def ghost_row(pair, x):
    source = pair[x % 2]
    return pltpu.roll(source, (LANES - DEPTH * x) % LANES, 1) if x else source


def lanes_beside(m, g, lane):
    first, last = lane == 0, lane == LANES - 1
    mp, gp = pltpu.roll(m, 1, 1), pltpu.roll(g, 1, 1)
    mn, gn = pltpu.roll(m, LANES - 1, 1), pltpu.roll(g, LANES - 1, 1)
    main = jnp.where(first, gp, mp) + jnp.where(last, gn, mn)
    ghost = jnp.where(first, mp, gp) + jnp.where(last, mn, gn)
    return main, ghost


def steps(shifts, wide, zr, zl, cm, cg, wm, wg, sm, sg, outs):
    lane = lax.broadcasted_iota(jnp.int32, (E, LANES), 1)
    slot = lane // DEPTH
    edge = jnp.zeros((1, LANES), F32)

    @pl.loop(0, 8)
    def _(f):
        pair = spread_ghosts(zr[f], zl[f], slot)
        for x in range(E):
            wg[f, x] = ghost_row(pair, x)

        @pl.loop(0, E)
        def _(x):
            for s in (sm, sg):
                s[f, x, PAD - 1 : PAD, :] = edge
                s[f, x, PAD + E : PAD + E + 1, :] = edge

    def inner(s, f, x):
        return s[f, x, PAD : PAD + E, :]

    for k, shift in enumerate(shifts):
        source = wide if k == 0 else wm

        @pl.loop(k, E - k)
        def _(x):
            for w, c, s in ((source, cm, sm), (wg, cg, sg)):
                p = [None] * LEVELS
                carry = None
                for t in range(LEVELS - 1, -1, -1):
                    top = w[t, x]
                    carry = (top if carry is None else top + carry) * c[t, x]
                    p[t] = carry
                    s[t, x, PAD : PAD + E, :] = carry
                carry = None
                for t in range(LEVELS):
                    top = w[LEVELS + t, x] + (6.0 * c[4 + t, x]) * p[t]
                    carry = (top if carry is None else top + carry) * c[t, x]
                    s[LEVELS + t, x, PAD : PAD + E, :] = carry

        last = k == len(shifts) - 1

        @pl.loop(k + 1, E - k - 1)
        def _(x):
            y0, rows = (DEPTH, N) if last else (0, E)
            span = slice(y0, y0 + rows)
            near = lane[:rows]

            def total(s, f, beside):
                rowsum = s[f, x - 1, PAD + y0 : PAD + y0 + rows, :] + s[f, x + 1, PAD + y0 : PAD + y0 + rows, :]
                rowsum = rowsum + s[f, x, PAD + y0 - 1 : PAD + y0 + rows - 1, :]
                rowsum = rowsum + s[f, x, PAD + y0 + 1 : PAD + y0 + rows + 1, :]
                return rowsum + beside

            for t in range(LEVELS):
                fields = []
                for f in (t, LEVELS + t):
                    m, g = (s[f, x, PAD + y0 : PAD + y0 + rows, :] for s in (sm, sg))
                    bm, bg = lanes_beside(m, g, near)
                    fields.append((m, g, bm, bg))
                columns = ((source, wm, cm, sm, 0), (wg, wg, cg, sg, 1))
                for w, to, c, s, col in columns[: 1 if last else 2]:
                    sp = total(s, t, fields[0][2 + col])
                    sr = total(s, LEVELS + t, fields[1][2 + col])
                    first = sp + c[8 + t, x, span, :] * fields[1][col]
                    second = sr - c[4 + t, x, span, :] * sp
                    if shift:
                        first = first + shift * w[t, x, span, :]
                        second = second + shift * w[LEVELS + t, x, span, :]
                    first, second = first * (-1.0 / SPREAD), second * (-1.0 / SPREAD)
                    if last:
                        outs[k][t, x - DEPTH] = first
                        outs[k][LEVELS + t, x - DEPTH] = second
                    else:
                        to[t, x] = first
                        to[LEVELS + t, x] = second

        if not last:
            @pl.loop(0, N)
            def _(x):
                for f in range(8):
                    outs[k][f, x] = wm[f, x + DEPTH, DEPTH : DEPTH + N, :]


def first_kernel(wide, zr, zl, cm, cg, *refs):
    place = [lax.axis_index("gx"), lax.axis_index("gy"), lax.axis_index(GZ)]
    outs, (wm, wg, sm, sg) = refs[:DEPTH], refs[DEPTH:]
    lane = lax.broadcasted_iota(jnp.int32, (E, LANES), 1)
    row = lax.broadcasted_iota(jnp.int32, (E, LANES), 0)
    slot = lane // DEPTH
    y_in = ((place[1] > 0) | (row >= DEPTH)) & ((place[1] < 3) | (row < DEPTH + N))
    z_in = ((lane < DEPTH) & (place[2] < 7)) | ((lane >= LANES - DEPTH) & (place[2] > 0))
    ym = y_in.astype(F32)
    yg = (y_in & z_in).astype(F32)

    @pl.loop(0, LEVELS)
    def _(f):
        pairs = [spread_ghosts(zr[b + f], zl[b + f], slot) for b in (8, 12, 16)]
        for x in range(E):
            inside = True
            if x < DEPTH:
                inside = place[0] > 0
            if x >= DEPTH + N:
                inside = place[0] < 3
            inside = jnp.where(inside, 1.0, 0.0).astype(F32) if inside is not True else 1.0
            cm[f, x] = (ym * inside) / (7.0 + wide[8 + f, x])
            cg[f, x] = (yg * inside) / (7.0 + ghost_row(pairs[0], x))
            for n in (1, 2):
                cm[4 * n + f, x] = wide[8 + 4 * n + f, x]
                cg[4 * n + f, x] = ghost_row(pairs[n], x)

    steps(SHIFT[:DEPTH], wide, zr, zl, cm, cg, wm, wg, sm, sg, outs)


def second_kernel(wide, zr, zl, cm, cg, *refs):
    outs, (wm, wg, sm, sg) = refs[:DEPTH], refs[DEPTH:]
    steps(SHIFT[DEPTH:], wide, zr, zl, cm, cg, wm, wg, sm, sg, outs)


def gram_kernel(*refs):
    vectors, out = refs[:VECTORS], refs[VECTORS]
    for low in range(0, len(PAIRS), 23):
        part = PAIRS[low : low + 23]
        used = sorted({v for pair in part for v in pair})

        def add(i, sums):
            held = {v: vectors[v][i // N, i % N] for v in used}
            new = []
            for (a, b), total in zip(part, sums):
                product = held[a] * held[b]
                new.append(total + (product[:8] + product[8:]))
            return tuple(new)

        sums = lax.fori_loop(0, 8 * N, add, tuple(jnp.zeros((8, LANES), F32) for _ in part))
        for n, total in enumerate(sums):
            out[low + n : low + n + 1, :] = jnp.sum(total, axis=0, keepdims=True)
    out[len(PAIRS) :, :] = jnp.zeros((ROWS - len(PAIRS), LANES), F32)


def solve(gram):
    entry = {pair: gram[n : n + 1] for n, pair in enumerate(PAIRS)}
    upper = {}
    for i in range(VECTORS):
        pivot = entry[i, i]
        for m in range(i):
            pivot = pivot - upper[m, i] * upper[m, i]
        pivot = jnp.maximum(pivot, 1e-7 * entry[i, i])
        root = jnp.sqrt(pivot)
        upper[i, i] = root
        for j in range(i + 1, VECTORS):
            value = entry[i, j]
            for m in range(i):
                value = value - upper[m, i] * upper[m, j]
            upper[i, j] = value / root
    columns = []
    for c in range(ITERS):
        column = [(1.0 + SHIFT[c]) * upper[i, c] + SPREAD * upper[i, c + 1] for i in range(c + 1)]
        columns.append(column + [SPREAD * upper[c + 1, c + 1]])
    return least_squares(columns, upper[0, 0], ITERS)


def least_squares(columns, beta, steps):
    rotations = []
    target = [beta] + [jnp.zeros_like(beta)] * steps
    upper = []
    for column_index in range(steps):
        column = list(columns[column_index])
        for place, (cosine, sine) in enumerate(rotations):
            upper_entry = cosine * column[place] + sine * column[place + 1]
            lower_entry = -sine * column[place] + cosine * column[place + 1]
            column[place], column[place + 1] = (upper_entry, lower_entry)
        radius = jnp.sqrt(column[column_index] ** 2 + column[column_index + 1] ** 2)
        cosine = column[column_index] / radius
        sine = column[column_index + 1] / radius
        column[column_index] = radius
        rotations.append((cosine, sine))
        target[column_index], target[column_index + 1] = (
            cosine * target[column_index],
            -sine * target[column_index],
        )
        upper.append(column[: column_index + 1])
    solved = [None] * steps
    for row_index in range(steps - 1, -1, -1):
        accum = target[row_index]
        for later_index in range(row_index + 1, steps):
            accum = accum - upper[later_index][row_index] * solved[later_index]
        solved[row_index] = accum / upper[row_index][row_index]
    return solved


def update_kernel(gram, rea, tra, *refs):
    vectors, out = refs[:ITERS], refs[ITERS]
    whole = jnp.broadcast_to(jnp.sum(gram[...], axis=1, keepdims=True), (ROWS, LANES))
    weights = [jnp.broadcast_to(row, (N, LANES)) for row in solve(whole)]

    @pl.loop(0, N)
    def _(x):
        def mixed(f):
            total = weights[0] * vectors[0][f, x]
            for weight, vector in zip(weights[1:], vectors[1:]):
                total = total + weight * vector[f, x]
            return total

        inverse = [1.0 / (7.0 + rea[t, x]) for t in range(LEVELS)]
        p = [None] * LEVELS
        carry = None
        for t in range(LEVELS - 1, -1, -1):
            top = mixed(t)
            carry = (top if carry is None else top + carry) * inverse[t]
            p[t] = carry
            out[t, x] = carry
        carry = None
        for t in range(LEVELS):
            top = mixed(LEVELS + t) + 6.0 * tra[t, x] * p[t]
            carry = (top if carry is None else top + carry) * inverse[t]
            out[LEVELS + t, x] = carry


def exchange(slabs):
    received = []
    for slab, (dx, dy) in zip(slabs, WAYS):
        pairs = [(x * 4 + y, (x + dx) % 4 * 4 + (y + dy) % 4) for x in range(4) for y in range(4)]
        received.append(lax.ppermute(slab, ("gx", "gy"), pairs))
    return received


def exchange_z(low, high):
    from_above = lax.ppermute(low, GZ, [((i + 1) % 8, i) for i in range(8)])
    from_below = lax.ppermute(high, GZ, [(i, (i + 1) % 8) for i in range(8)])
    return from_above, from_below


def add_up(part):
    for axis in ("gz_1", "gx", "gy", "gz_0"):
        size = lax.axis_size(axis)
        got = [lax.ppermute(part, axis, [(i, i ^ d) for i in range(size)]) for d in range(1, size)]
        part = part + got[0] if size == 2 else (part + got[0]) + (got[1] + got[2])
    return part


def body(residual_in, reaction, transport, congestion):
    res = residual_in.reshape(8, N, N, LANES)
    core = (8, N, N, LANES)
    scratch = [vmem((8, E, E, LANES))] * 2 + [vmem((8, E, E + 2 * PAD, LANES))] * 2
    shape = lambda *s: jax.ShapeDtypeStruct(s, F32)

    slabs = call(pack_kernel, [shape(*slab_shape(20, w)) for w in WAYS], res, reaction, transport, congestion)
    slabs = exchange(slabs)
    wide, low, high = call(
        functools.partial(widen_kernel, 4),
        [vmem((20, E, E, LANES)), shape(20, E, LANES), shape(20, E, LANES)],
        res, reaction, transport, congestion, *slabs,
    )
    zr, zl = exchange_z(low, high)
    cm, cg, *made = call(
        first_kernel,
        [vmem((12, E, E, LANES))] * 2 + [vmem(core)] * DEPTH,
        wide, zr, zl, scratch=scratch,
    )
    slabs = call(slab_kernel, [shape(*slab_shape(8, w)) for w in WAYS], made[-1])
    slabs = exchange(slabs)
    wide, low, high = call(
        functools.partial(widen_kernel, 1),
        [vmem((8, E, E, LANES)), shape(8, E, LANES), shape(8, E, LANES)],
        made[-1], *slabs,
    )
    zr, zl = exchange_z(low, high)
    more = call(second_kernel, [vmem(core)] * DEPTH, wide, zr, zl, cm, cg, scratch=scratch)
    basis = [res] + list(made) + list(more)
    part, = call(gram_kernel, [shape(ROWS, LANES)], *basis)
    gram = add_up(part)
    out, = call(update_kernel, [shape(*core)], gram, reaction, transport, *basis[:ITERS])
    return out.reshape(residual_in.shape)


def solution(mesh):
    torus = Mesh(
        mesh.devices.reshape(mesh.shape["gx"], mesh.shape["gy"], 4, 2), ("gx", "gy", "gz_0", "gz_1")
    )
    field = P(None, "gx", "gy", GZ)
    pair = P(None, None, "gx", "gy", GZ)
    return jax.shard_map(
        body, mesh=torus, in_specs=(pair, field, field, field), out_specs=pair, check_vma=False
    )
```

```python
import functools

import jax
import jax.numpy as jnp
from jax import lax
from jax.experimental import pallas as pl
from jax.experimental.pallas import tpu as pltpu
from jax.sharding import Mesh
from jax.sharding import PartitionSpec as P

ITERS = 8
LEVELS = 4
DEPTH = 4
N = 16
E = N + 2 * DEPTH
LANES = 128
PAD = 8
VECTORS = ITERS + 1
PAIRS = [(i, j) for j in range(VECTORS) for i in range(j + 1)]
EARLY = 15
ROWS = 48
GZ = ("gz_0", "gz_1")
SHIFT = (0.68, -0.68, 0.0, -0.392, 0.448, -0.57, 0.592, 0.208)
F32 = jnp.float32


def vmem(shape):
    return pltpu.VMEM(shape, F32)


def call(kernel, outs, *args, scratch=(), far=False, alias=None, cost=1000000):
    whole = pl.BlockSpec(memory_space=pltpu.VMEM)
    return pl.pallas_call(
        kernel,
        out_shape=outs,
        in_specs=[pl.BlockSpec(memory_space=pltpu.HBM) if far else whole] * len(args),
        out_specs=[whole] * len(outs),
        scratch_shapes=list(scratch),
        input_output_aliases=alias or {},
        compiler_params=pltpu.CompilerParams(vmem_limit_bytes=LIMIT),
        cost_estimate=pl.CostEstimate(flops=cost, bytes_accessed=cost, transcendentals=0),
    )(*args)


LIMIT = 24 * 1024 * 1024
SLAB = {
    (-1, 0): (slice(0, DEPTH), slice(0, N)),
    (1, 0): (slice(N - DEPTH, N), slice(0, N)),
    (0, -1): (slice(0, N), slice(0, DEPTH)),
    (0, 1): (slice(0, N), slice(N - DEPTH, N)),
}
CORNERS = [(-1, -1), (1, 1), (-1, 1), (1, -1)]
STEPS_OUT = [(a, b) for a in range(1, DEPTH) for b in range(1, DEPTH) if a + b <= DEPTH]
WAYS = list(SLAB) + CORNERS


def landing(way):
    low = lambda d: DEPTH if d == 0 else (0 if d > 0 else DEPTH + N)
    size = lambda d: N if d == 0 else DEPTH
    return tuple(slice(low(d), low(d) + size(d)) for d in way)


def slab_shape(fields, way):
    if way in CORNERS:
        return (fields, len(STEPS_OUT), LANES)
    return (fields,) + tuple(N if d == 0 else DEPTH for d in way) + (LANES,)


def cut(core, f, outs, to):
    for out, way in zip(outs, WAYS):
        if way in SLAB:
            xs, ys = SLAB[way]
            out[to, :, :, :] = core[f, xs, ys, :]
        else:
            for n, (a, b) in enumerate(STEPS_OUT):
                x, y = (N - c if d > 0 else c - 1 for c, d in zip((a, b), way))
                out[to, n : n + 1, :] = core[f, x, y : y + 1, :]


def fill(wide, f, slabs):
    for slab, way in zip(slabs, WAYS):
        if way in SLAB:
            xs, ys = landing(way)
            wide[f, xs, ys, :] = slab[f]
        else:
            for n, (a, b) in enumerate(STEPS_OUT):
                x, y = (DEPTH - c if d > 0 else DEPTH + N + c - 1 for c, d in zip((a, b), way))
                wide[f, x, y : y + 1, :] = slab[f, n : n + 1, :]


def pack_kernel(res, rea, tra, con, *refs):
    slabs, held, done = refs[:8], refs[8:12], refs[12]
    copies = [pltpu.make_async_copy(src, dst, done.at[n]) for n, (src, dst) in enumerate(zip((res, rea, tra, con), held))]
    for copy in copies:
        copy.start()
    for copy, source, base in zip(copies, held, (0, 8, 12, 16)):
        copy.wait()

        @pl.loop(0, source.shape[0])
        def _(f):
            cut(source, f, slabs, base + f)


def slab_kernel(core, *outs):
    @pl.loop(0, 8)
    def _(f):
        cut(core, f, outs, f)


def core_kernel(*refs):
    cores, wide = refs[:-1], refs[-1]
    base = 0
    for core in cores:
        count = core.shape[0]

        @pl.loop(0, count)
        def _(f):
            for side in (0, DEPTH + N):
                wide[base + f, side : side + DEPTH] = jnp.zeros((DEPTH, E, LANES), F32)
            wide[base + f, DEPTH : DEPTH + N, DEPTH : DEPTH + N, :] = core[f]

        base = base + count


def widen_kernel(given, *refs):
    slabs, (wide, low, high) = refs[:8], refs[8:]
    slot = lax.broadcasted_iota(jnp.int32, (E, LANES), 1) // DEPTH

    @pl.loop(0, wide.shape[0])
    def _(f):
        fill(wide, f, slabs)
        lo = jnp.zeros((E, LANES), F32)
        hi = jnp.zeros((E, LANES), F32)
        for x in range(E):
            rolled = pltpu.roll(wide[f, x], DEPTH * x, 1) if x else wide[f, x]
            lo = jnp.where(slot == x, rolled, lo)
            hi = jnp.where(slot == (x - 1) % (LANES // DEPTH), rolled, hi)
        low[f] = lo
        high[f] = pltpu.roll(hi, DEPTH, 1)


def weights_kernel(out):
    i = lax.broadcasted_iota(jnp.int32, (2 * LANES, 2 * LANES), 0)
    j = lax.broadcasted_iota(jnp.int32, (2 * LANES, 2 * LANES), 1)
    inside = (i < LANES) & (j < LANES) & ((i - j == 1) | (j - i == 1))

    @pl.loop(0, E)
    def _(x):
        slot = LANES + DEPTH * x
        above = ((i == LANES - 1) & (j == slot)) | ((i == slot) & (j == LANES - 1))
        below = ((i == 0) & (j == slot + 1)) | ((i == slot + 1) & (j == 0))
        out[x] = (inside | above | below).astype(F32).astype(jnp.bfloat16)


def thirds(value):
    parts = []
    for _ in range(3):
        part = value.astype(jnp.bfloat16)
        parts.append(part)
        value = value - part.astype(F32)
    return parts


def steps(shifts, wide, ghosts, inv, coefs, ginv, gcoefs, select, wm, sm, gw, gs, along_z, ends, outs):
    lane = lax.broadcasted_iota(jnp.int32, (E, LANES), 1)
    place = lane % DEPTH
    wider = lax.broadcasted_iota(jnp.int32, (8 * E, LANES), 1)
    none = jnp.zeros((1, LANES), F32)

    @pl.loop(0, 8)
    def _(f):
        for x in range(E):
            sm[f, x, PAD - 1 : PAD, :] = none
            sm[f, x, PAD + E : PAD + E + 1, :] = none
        for side in range(2):
            gs[side, f, PAD - 1 : PAD, :] = none
            gs[side, f, PAD + E : PAD + E + 1, :] = none

    def precondition(w, v, transport, store):
        p = [None] * LEVELS
        carry = None
        for t in range(LEVELS - 1, -1, -1):
            top = w(t)
            carry = (top if carry is None else top + carry) * v(t)
            p[t] = carry
            store(t, carry)
        carry = None
        for t in range(LEVELS):
            top = w(LEVELS + t) + (6.0 * transport(t)) * p[t]
            carry = (top if carry is None else top + carry) * v(t)
            store(LEVELS + t, carry)

    middle = slice(PAD, PAD + E)
    for k, shift in enumerate(shifts):
        source = wide if k == 0 else wm
        beyond = [ghosts[side] if k == 0 else gw.at[side] for side in range(2)]
        final = k == len(shifts) - 1

        @pl.loop(k, E - k)
        def _(x):
            def store(f, value):
                sm[f, x, middle, :] = value

            precondition(lambda f: source[f, x], lambda t: inv[t, x], lambda t: coefs[t, x], store)

        for side in range(2):
            def store(f, value):
                gs[side, f, middle, :] = value

            precondition(lambda f: beyond[side][f], lambda t: ginv[side, t], lambda t: gcoefs[side, t], store)

        lower = pltpu.roll(gs[1, :, middle, :].reshape(8 * E, LANES), LANES - 2, 1)
        over = jnp.where(wider % DEPTH == 1, lower, gs[0, :, middle, :].reshape(8 * E, LANES))
        outer = jnp.concatenate(thirds(over), axis=0)
        ends[...] = jnp.zeros_like(ends)

        group = (E - 2 * k - 2) // 2

        @pl.loop(0, 2)
        def _(n):
            packed = None
            for m in range(group):
                x = k + 1 + n * group + m
                parts = thirds(sm[:, x, middle, :].reshape(8 * E, LANES))
                both = jnp.concatenate([jnp.concatenate(parts, axis=0), outer], axis=1)
                moved = jnp.dot(both, select[x], preferred_element_type=F32)
                rows = [moved[8 * E * i : 8 * E * (i + 1)] for i in range(len(parts))]
                total = functools.reduce(lambda a, b: a + b, rows)
                along_z[:, x] = total[:, :LANES].reshape(8, E, LANES)
                packed = total[:, LANES:] if packed is None else packed + total[:, LANES:]
            ends[...] += packed.reshape(8, E, LANES)

        def beside_ghost(f):
            inner = ends[f]
            sums = []
            for side in range(2):
                value = gs[side, f, middle, :]
                before, after = pltpu.roll(value, 1, 1), pltpu.roll(value, LANES - 1, 1)
                if side == 0:
                    before = jnp.where(place == 0, inner, before)
                else:
                    after = jnp.where(place == DEPTH - 1, pltpu.roll(inner, 2, 1), after)
                total = before + after + gs[side, f, PAD - 1 : PAD + E - 1, :] + gs[side, f, PAD + 1 : PAD + E + 1, :]
                sums.append(total + pltpu.roll(value, DEPTH, 1) + pltpu.roll(value, LANES - DEPTH, 1))
            return sums

        if not final:
            @pl.loop(0, LEVELS)
            def _(t):
                p_sums, r_sums = beside_ghost(t), beside_ghost(LEVELS + t)
                for side in range(2):
                    first = p_sums[side] + gcoefs[side, LEVELS + t] * gs[side, LEVELS + t, middle, :]
                    second = r_sums[side] - gcoefs[side, t] * p_sums[side]
                    if shift:
                        first = first + shift * beyond[side][t]
                        second = second + shift * beyond[side][LEVELS + t]
                    gw[side, t] = first
                    gw[side, LEVELS + t] = second

        y0, rows = (DEPTH, N) if final else (0, E)
        span = slice(y0, y0 + rows)

        @pl.loop(k + 1, E - k - 1)
        def _(x):
            def around(f):
                across = sm[f, x - 1, PAD + y0 : PAD + y0 + rows, :] + sm[f, x + 1, PAD + y0 : PAD + y0 + rows, :]
                along = sm[f, x, PAD + y0 - 1 : PAD + y0 + rows - 1, :] + sm[f, x, PAD + y0 + 1 : PAD + y0 + rows + 1, :]
                return along_z[f, x, span, :] + (across + along)

            for t in range(LEVELS):
                sp, sr = around(t), around(LEVELS + t)
                r = sm[LEVELS + t, x, PAD + y0 : PAD + y0 + rows, :]
                first = sp + coefs[LEVELS + t, x, span, :] * r
                second = sr - coefs[t, x, span, :] * sp
                if shift:
                    first = first + shift * source[t, x, span, :]
                    second = second + shift * source[LEVELS + t, x, span, :]
                if final:
                    outs[k][t, x - DEPTH] = first
                    outs[k][LEVELS + t, x - DEPTH] = second
                else:
                    wm[t, x] = first
                    wm[LEVELS + t, x] = second

        if not final:
            @pl.loop(0, N)
            def _(x):
                for f in range(8):
                    outs[k][f, x] = wm[f, x + DEPTH, DEPTH : DEPTH + N, :]


def first_kernel(wide, upper, lower, select, inv, ginv, gcoefs, *refs):
    outs, scratch = refs[:DEPTH], refs[DEPTH:]
    place = [lax.axis_index("gx"), lax.axis_index("gy"), lax.axis_index(GZ)]
    lane = lax.broadcasted_iota(jnp.int32, (E, LANES), 1)
    row = lax.broadcasted_iota(jnp.int32, (E, LANES), 0)
    slot = lane // DEPTH

    def within(index, spot):
        return (index < E) & ((spot > 0) | (index >= DEPTH)) & ((spot < 3) | (index < DEPTH + N))

    y_in = within(row, place[1])
    ym = y_in.astype(F32)
    xy = (y_in & within(slot, place[0])).astype(F32)
    ends = ((place[2] < 7).astype(F32), (place[2] > 0).astype(F32))

    @pl.loop(0, E)
    def _(x):
        mask = ym * within(x, place[0]).astype(F32)
        for t in range(LEVELS):
            inv[t, x] = mask / (7.0 + wide[8 + t, x])

    for side, ghost in enumerate((upper, lower)):
        for t in range(LEVELS):
            ginv[side, t] = (xy * ends[side]) / (7.0 + ghost[8 + t])
            gcoefs[side, t] = ghost[12 + t]
            gcoefs[side, LEVELS + t] = ghost[16 + t]

    steps(SHIFT[:DEPTH], wide, (upper, lower), inv, wide.at[12:20], ginv, gcoefs, select, *scratch, outs)


def second_kernel(wide, upper, lower, select, inv, coefs, ginv, gcoefs, *refs):
    outs, scratch = refs[:DEPTH], refs[DEPTH:]
    steps(SHIFT[DEPTH:], wide, (upper, lower), inv, coefs.at[12:20], ginv, gcoefs, select, *scratch, outs)


def products(vectors, pairs):
    used = sorted({v for pair in pairs for v in pair})

    def add(i, sums):
        held = {v: vectors[v][i // N, i % N] for v in used}
        new = []
        for (a, b), total in zip(pairs, sums):
            product = held[a] * held[b]
            new.append(total + (product[:8] + product[8:]))
        return tuple(new)

    sums = lax.fori_loop(0, 8 * N, add, tuple(jnp.zeros((8, LANES), F32) for _ in pairs))
    return [jnp.sum(total, axis=0, keepdims=True) for total in sums]


def early_gram_kernel(*refs):
    vectors, out = refs[:-1], refs[-1]
    for n, row in enumerate(products(vectors, PAIRS[:EARLY])):
        out[n : n + 1, :] = row
    out[EARLY:, :] = jnp.zeros((1, LANES), F32)


def gram_kernel(early, *refs):
    vectors, out = refs[:-1], refs[-1]
    out[:EARLY, :] = early[:EARLY, :]
    for n, row in enumerate(products(vectors, PAIRS[EARLY:])):
        out[EARLY + n : EARLY + n + 1, :] = row
    out[len(PAIRS) :, :] = jnp.zeros((ROWS - len(PAIRS), LANES), F32)


def solve(gram):
    entry = {pair: gram[n : n + 1] for n, pair in enumerate(PAIRS)}
    upper = {}
    for i in range(VECTORS):
        pivot = entry[i, i]
        for m in range(i):
            pivot = pivot - upper[m, i] * upper[m, i]
        pivot = jnp.maximum(pivot, 1e-7 * entry[i, i])
        root = jnp.sqrt(pivot)
        upper[i, i] = root
        for j in range(i + 1, VECTORS):
            value = entry[i, j]
            for m in range(i):
                value = value - upper[m, i] * upper[m, j]
            upper[i, j] = value / root
    columns = []
    for c in range(ITERS):
        column = [(1.0 + SHIFT[c]) * upper[i, c] - upper[i, c + 1] for i in range(c + 1)]
        columns.append(column + [-upper[c + 1, c + 1]])
    return least_squares(columns, upper[0, 0], ITERS)


def least_squares(columns, beta, steps):
    rotations = []
    target = [beta] + [jnp.zeros_like(beta)] * steps
    upper = []
    for column_index in range(steps):
        column = list(columns[column_index])
        for place, (cosine, sine) in enumerate(rotations):
            upper_entry = cosine * column[place] + sine * column[place + 1]
            lower_entry = -sine * column[place] + cosine * column[place + 1]
            column[place], column[place + 1] = (upper_entry, lower_entry)
        radius = jnp.sqrt(column[column_index] ** 2 + column[column_index + 1] ** 2)
        cosine = column[column_index] / radius
        sine = column[column_index + 1] / radius
        column[column_index] = radius
        rotations.append((cosine, sine))
        target[column_index], target[column_index + 1] = (
            cosine * target[column_index],
            -sine * target[column_index],
        )
        upper.append(column[: column_index + 1])
    solved = [None] * steps
    for row_index in range(steps - 1, -1, -1):
        accum = target[row_index]
        for later_index in range(row_index + 1, steps):
            accum = accum - upper[later_index][row_index] * solved[later_index]
        solved[row_index] = accum / upper[row_index][row_index]
    return solved


def update_kernel(gram, rea, tra, *refs):
    vectors, out = refs[:ITERS], refs[ITERS]
    whole = jnp.broadcast_to(jnp.sum(gram[...], axis=1, keepdims=True), (ROWS, LANES))
    weights = [jnp.broadcast_to(row, (N, LANES)) for row in solve(whole)]

    @pl.loop(0, N)
    def _(x):
        def mixed(f):
            total = weights[0] * vectors[0][f, x]
            for weight, vector in zip(weights[1:], vectors[1:]):
                total = total + weight * vector[f, x]
            return total

        inverse = [1.0 / (7.0 + rea[t, x]) for t in range(LEVELS)]
        p = [None] * LEVELS
        carry = None
        for t in range(LEVELS - 1, -1, -1):
            top = mixed(t)
            carry = (top if carry is None else top + carry) * inverse[t]
            p[t] = carry
            out[t, x] = carry
        carry = None
        for t in range(LEVELS):
            top = mixed(LEVELS + t) + 6.0 * tra[t, x] * p[t]
            carry = (top if carry is None else top + carry) * inverse[t]
            out[LEVELS + t, x] = carry


def exchange(slabs):
    received = []
    for slab, (dx, dy) in zip(slabs, WAYS):
        pairs = [(x * 4 + y, (x + dx) % 4 * 4 + (y + dy) % 4) for x in range(4) for y in range(4)]
        received.append(lax.ppermute(slab, ("gx", "gy"), pairs))
    return received


def exchange_z(low, high):
    from_above = lax.ppermute(low, GZ, [((i + 1) % 8, i) for i in range(8)])
    from_below = lax.ppermute(high, GZ, [(i, (i + 1) % 8) for i in range(8)])
    return from_above, from_below


def add_up(part):
    for axis in ("gz_1", "gx", "gy", "gz_0"):
        size = lax.axis_size(axis)
        got = [lax.ppermute(part, axis, [(i, i ^ d) for i in range(size)]) for d in range(1, size)]
        part = part + got[0] if size == 2 else (part + got[0]) + (got[1] + got[2])
    return part


def body(residual_in, reaction, transport, congestion):
    given = (residual_in.reshape(8, N, N, LANES), reaction, transport, congestion)
    given = [pltpu.with_memory_space_constraint(g, pltpu.HBM) for g in given]
    core, half, packed = (8, N, N, LANES), (4, N, N, LANES), (E, LANES)
    scratch = [vmem((8, E, E, LANES)), vmem((8, E, E + 2 * PAD, LANES)), vmem((2, 8) + packed)]
    scratch += [vmem((2, 8, E + 2 * PAD, LANES))]
    scratch += [vmem((8, E, E, LANES)), vmem((8,) + packed)]
    shape = lambda *s: jax.ShapeDtypeStruct(s, F32)

    def surround(slabs, held):
        fields = sum(h.shape[0] for h in held)
        received = exchange(slabs)
        inside, = call(core_kernel, [vmem((fields, E, E, LANES))], *held)
        wide, low, high = call(
            widen_kernel,
            [vmem((fields, E, E, LANES)), shape(fields, *packed), shape(fields, *packed)],
            inside, *received, alias={0: 0},
        )
        return wide, *exchange_z(low, high)

    *slabs, res, rea, tra, con = call(
        pack_kernel,
        [shape(*slab_shape(20, w)) for w in WAYS] + [vmem(core)] + [vmem(half)] * 3,
        *given, far=True, scratch=[pltpu.SemaphoreType.DMA((4,))],
    )
    select, = call(weights_kernel, [pltpu.VMEM((E, 2 * LANES, 2 * LANES), jnp.bfloat16)])
    fields, upper, lower = surround(slabs, (res, rea, tra, con))
    inv, ginv, gcoefs, *made = call(
        first_kernel,
        [vmem((4, E, E, LANES)), vmem((2, 4) + packed), vmem((2, 8) + packed)] + [vmem(core)] * DEPTH,
        fields, upper, lower, select, scratch=scratch,
    )
    slabs = call(slab_kernel, [shape(*slab_shape(8, w)) for w in WAYS], made[-1])
    early, = call(early_gram_kernel, [vmem((EARLY + 1, LANES))], res, *made)
    wide, upper, lower = surround(slabs, made[-1:])
    more = call(second_kernel, [vmem(core)] * DEPTH, wide, upper, lower, select, inv, fields, ginv, gcoefs, scratch=scratch)
    basis = [res] + list(made) + list(more)
    part, = call(gram_kernel, [shape(ROWS, LANES)], early, *basis)
    gram = add_up(part)
    out, = call(update_kernel, [shape(*core)], gram, rea, tra, *basis[:ITERS])
    return out.reshape(residual_in.shape)


def solution(mesh):
    torus = Mesh(
        mesh.devices.reshape(mesh.shape["gx"], mesh.shape["gy"], 4, 2), ("gx", "gy", "gz_0", "gz_1")
    )
    field = P(None, "gx", "gy", GZ)
    pair = P(None, None, "gx", "gy", GZ)
    return jax.shard_map(
        body, mesh=torus, in_specs=(pair, field, field, field), out_specs=pair, check_vma=False
    )
```

```python
import functools

import jax
import jax.numpy as jnp
from jax import lax
from jax.experimental import pallas as pl
from jax.experimental.pallas import tpu as pltpu
from jax.sharding import Mesh
from jax.sharding import PartitionSpec as P

ITERS = 8
LEVELS = 4
DEPTH = 4
N = 16
E = N + 2 * DEPTH
LANES = 128
PAD = 8
VECTORS = ITERS + 1
PAIRS = [(i, j) for j in range(VECTORS) for i in range(j + 1)]
EARLY = 15
ROWS = 48
GZ = ("gz_0", "gz_1")
GX_GY_GZ = ("gx", "gy", "gz_0", "gz_1")
THIN = 1e-5
SHIFT = (0.68, -0.68, 0.0, -0.392, 0.448, -0.57, 0.592, 0.208)
F32 = jnp.float32


def vmem(shape):
    return pltpu.VMEM(shape, F32)


def call(kernel, outs, *args, scratch=(), far=False, alias=None, cost=1000000):
    whole = pl.BlockSpec(memory_space=pltpu.VMEM)
    return pl.pallas_call(
        kernel,
        out_shape=outs,
        in_specs=[pl.BlockSpec(memory_space=pltpu.HBM) if far else whole] * len(args),
        out_specs=[whole] * len(outs),
        scratch_shapes=list(scratch),
        input_output_aliases=alias or {},
        compiler_params=pltpu.CompilerParams(vmem_limit_bytes=LIMIT),
        cost_estimate=pl.CostEstimate(flops=cost, bytes_accessed=cost, transcendentals=0),
    )(*args)


LIMIT = 24 * 1024 * 1024
SLAB = {
    (-1, 0): (slice(0, DEPTH), slice(0, N)),
    (1, 0): (slice(N - DEPTH, N), slice(0, N)),
    (0, -1): (slice(0, N), slice(0, DEPTH)),
    (0, 1): (slice(0, N), slice(N - DEPTH, N)),
}
CORNERS = [(-1, -1), (1, 1), (-1, 1), (1, -1)]
STEPS_OUT = [(a, b) for a in range(1, DEPTH) for b in range(1, DEPTH) if a + b <= DEPTH]
WAYS = list(SLAB) + CORNERS


def landing(way):
    low = lambda d: DEPTH if d == 0 else (0 if d > 0 else DEPTH + N)
    size = lambda d: N if d == 0 else DEPTH
    return tuple(slice(low(d), low(d) + size(d)) for d in way)


def slab_shape(fields, way):
    if way in CORNERS:
        return (fields, len(STEPS_OUT), LANES)
    return (fields,) + tuple(N if d == 0 else DEPTH for d in way) + (LANES,)


def cut(core, f, outs, to):
    for out, way in zip(outs, WAYS):
        if way in SLAB:
            xs, ys = SLAB[way]
            out[to, :, :, :] = core[f, xs, ys, :]
        else:
            for n, (a, b) in enumerate(STEPS_OUT):
                x, y = (N - c if d > 0 else c - 1 for c, d in zip((a, b), way))
                out[to, n : n + 1, :] = core[f, x, y : y + 1, :]


def fill(wide, f, slabs):
    for slab, way in zip(slabs, WAYS):
        if way in SLAB:
            xs, ys = landing(way)
            wide[f, xs, ys, :] = slab[f]
        else:
            for n, (a, b) in enumerate(STEPS_OUT):
                x, y = (DEPTH - c if d > 0 else DEPTH + N + c - 1 for c, d in zip((a, b), way))
                wide[f, x, y : y + 1, :] = slab[f, n : n + 1, :]


def pack_kernel(res, rea, tra, con, *refs):
    slabs, held, done = refs[:8], refs[8:12], refs[12]
    copies = [pltpu.make_async_copy(src, dst, done.at[n]) for n, (src, dst) in enumerate(zip((res, rea, tra, con), held))]
    for copy in copies:
        copy.start()
    for copy, source, base in zip(copies, held, (0, 8, 12, 16)):
        copy.wait()

        @pl.loop(0, source.shape[0])
        def _(f):
            cut(source, f, slabs, base + f)


def slab_kernel(core, *outs):
    @pl.loop(0, 8)
    def _(f):
        cut(core, f, outs, f)


def pack_rows(rows, shape):
    slot = lax.broadcasted_iota(jnp.int32, shape, 1) // DEPTH
    lo = hi = jnp.zeros(shape, F32)
    for x, value in rows:
        rolled = pltpu.roll(value, DEPTH * x, 1) if x else value
        lo = jnp.where(slot == x, rolled, lo)
        hi = jnp.where(slot == (x - 1) % (LANES // DEPTH), rolled, hi)
    return lo, pltpu.roll(hi, DEPTH, 1)


def core_kernel(*refs):
    cores, (wide, low, high) = refs[:-3], refs[-3:]
    base = 0
    for core in cores:
        count = core.shape[0]

        @pl.loop(0, count)
        def _(f):
            for side in (0, DEPTH + N):
                wide[base + f, side : side + DEPTH] = jnp.zeros((DEPTH, E, LANES), F32)
            wide[base + f, DEPTH : DEPTH + N, DEPTH : DEPTH + N, :] = core[f]
            low[base + f], high[base + f] = pack_rows([(x + DEPTH, core[f, x]) for x in range(N)], (N, LANES))

        base = base + count


def widen_kernel(given, core_low, core_high, *refs):
    slabs, (wide, low, high) = refs[:8], refs[8:]
    slot = lax.broadcasted_iota(jnp.int32, (8, LANES), 1) // DEPTH
    row = lax.broadcasted_iota(jnp.int32, (8, LANES), 0)
    middle = (slot >= DEPTH) & (slot < DEPTH + N)
    tall = lax.broadcasted_iota(jnp.int32, (N, LANES), 1) // DEPTH
    tall = (tall >= DEPTH) & (tall < DEPTH + N)

    def widen(f):
        fill(wide, f, slabs)
        outside = [x for x in range(E) if not DEPTH <= x < DEPTH + N]
        sides = pack_rows([(x, wide[f, x]) for x in outside], (E, LANES))
        beyond = [
            (x, jnp.where(row < DEPTH, wide[f, x, 0:8, :], wide[f, x, E - 8 : E, :]))
            for x in range(DEPTH, DEPTH + N)
        ]
        ends = pack_rows(beyond, (8, LANES))
        for out, side, end, core in zip((low, high), sides, ends, (core_low, core_high)):
            out[f, 0:8, :] = jnp.where(middle & (row < DEPTH), end, side[0:8])
            out[f, 8 : E - 8, :] = side[8 : E - 8]
            out[f, E - 8 : E, :] = jnp.where(middle & (row >= 8 - DEPTH), end, side[E - 8 : E])
            span = slice(DEPTH, DEPTH + N)
            out[f, span, :] = jnp.where(tall, core[f], side[span])

    @pl.loop(0, wide.shape[0] // 2)
    def _(n):
        widen(2 * n)
        widen(2 * n + 1)


def weights_kernel(out):
    i = lax.broadcasted_iota(jnp.int32, (2 * LANES, 2 * LANES), 0)
    j = lax.broadcasted_iota(jnp.int32, (2 * LANES, 2 * LANES), 1)
    inside = (i < LANES) & (j < LANES) & ((i - j == 1) | (j - i == 1))

    @pl.loop(0, E)
    def _(x):
        slot = LANES + DEPTH * x
        above = ((i == LANES - 1) & (j == slot)) | ((i == slot) & (j == LANES - 1))
        below = ((i == 0) & (j == slot + 1)) | ((i == slot + 1) & (j == 0))
        out[x] = (inside | above | below).astype(F32).astype(jnp.bfloat16)


def thirds(value):
    parts = []
    for _ in range(3):
        part = value.astype(jnp.bfloat16)
        parts.append(part)
        value = value - part.astype(F32)
    return parts


def steps(shifts, wide, ghosts, inv, coefs, ginv, gcoefs, select, wm, sm, gw, gs, along_z, ends, outs):
    lane = lax.broadcasted_iota(jnp.int32, (E, LANES), 1)
    place = lane % DEPTH
    wider = lax.broadcasted_iota(jnp.int32, (8 * E, LANES), 1)
    none = jnp.zeros((1, LANES), F32)

    @pl.loop(0, 8)
    def _(f):
        for x in range(E):
            sm[f, x, PAD - 1 : PAD, :] = none
            sm[f, x, PAD + E : PAD + E + 1, :] = none
        for side in range(2):
            gs[side, f, PAD - 1 : PAD, :] = none
            gs[side, f, PAD + E : PAD + E + 1, :] = none

    def precondition(w, v, transport, store):
        p = [None] * LEVELS
        carry = None
        for t in range(LEVELS - 1, -1, -1):
            top = w(t)
            carry = (top if carry is None else top + carry) * v(t)
            p[t] = carry
            store(t, carry)
        carry = None
        for t in range(LEVELS):
            top = w(LEVELS + t) + (6.0 * transport(t)) * p[t]
            carry = (top if carry is None else top + carry) * v(t)
            store(LEVELS + t, carry)

    middle = slice(PAD, PAD + E)
    for k, shift in enumerate(shifts):
        source = wide if k == 0 else wm
        beyond = [ghosts[side] if k == 0 else gw.at[side] for side in range(2)]
        final = k == len(shifts) - 1

        @pl.loop(k, E - k)
        def _(x):
            def store(f, value):
                sm[f, x, middle, :] = value

            precondition(lambda f: source[f, x], lambda t: inv[t, x], lambda t: coefs[t, x], store)

        for side in range(2):
            def store(f, value):
                gs[side, f, middle, :] = value

            precondition(lambda f: beyond[side][f], lambda t: ginv[side, t], lambda t: gcoefs[side, t], store)

        lower = pltpu.roll(gs[1, :, middle, :].reshape(8 * E, LANES), LANES - 2, 1)
        over = jnp.where(wider % DEPTH == 1, lower, gs[0, :, middle, :].reshape(8 * E, LANES))
        outer = jnp.concatenate(thirds(over), axis=0)
        ends[...] = jnp.zeros_like(ends)

        group = (E - 2 * k - 2) // 2

        @pl.loop(0, 2)
        def _(n):
            packed = None
            for m in range(group):
                x = k + 1 + n * group + m
                parts = thirds(sm[:, x, middle, :].reshape(8 * E, LANES))
                both = jnp.concatenate([jnp.concatenate(parts, axis=0), outer], axis=1)
                moved = jnp.dot(both, select[x], preferred_element_type=F32)
                rows = [moved[8 * E * i : 8 * E * (i + 1)] for i in range(len(parts))]
                total = functools.reduce(lambda a, b: a + b, rows)
                along_z[:, x] = total[:, :LANES].reshape(8, E, LANES)
                packed = total[:, LANES:] if packed is None else packed + total[:, LANES:]
            ends[...] += packed.reshape(8, E, LANES)

        def beside_ghost(f):
            inner = ends[f]
            sums = []
            for side in range(2):
                value = gs[side, f, middle, :]
                before, after = pltpu.roll(value, 1, 1), pltpu.roll(value, LANES - 1, 1)
                if side == 0:
                    before = jnp.where(place == 0, inner, before)
                else:
                    after = jnp.where(place == DEPTH - 1, pltpu.roll(inner, 2, 1), after)
                total = before + after + gs[side, f, PAD - 1 : PAD + E - 1, :] + gs[side, f, PAD + 1 : PAD + E + 1, :]
                sums.append(total + pltpu.roll(value, DEPTH, 1) + pltpu.roll(value, LANES - DEPTH, 1))
            return sums

        if not final:
            for t in range(LEVELS):
                p_sums, r_sums = beside_ghost(t), beside_ghost(LEVELS + t)
                for side in range(2):
                    first = p_sums[side] + gcoefs[side, LEVELS + t] * gs[side, LEVELS + t, middle, :]
                    second = r_sums[side] - gcoefs[side, t] * p_sums[side]
                    if shift:
                        first = first + shift * beyond[side][t]
                        second = second + shift * beyond[side][LEVELS + t]
                    gw[side, t] = first
                    gw[side, LEVELS + t] = second

        y0, rows = (DEPTH, N) if final else (0, E)
        span = slice(y0, y0 + rows)

        @pl.loop(k + 1, E - k - 1)
        def _(x):
            def around(f):
                across = sm[f, x - 1, PAD + y0 : PAD + y0 + rows, :] + sm[f, x + 1, PAD + y0 : PAD + y0 + rows, :]
                along = sm[f, x, PAD + y0 - 1 : PAD + y0 + rows - 1, :] + sm[f, x, PAD + y0 + 1 : PAD + y0 + rows + 1, :]
                return along_z[f, x, span, :] + (across + along)

            for t in range(LEVELS):
                sp, sr = around(t), around(LEVELS + t)
                r = sm[LEVELS + t, x, PAD + y0 : PAD + y0 + rows, :]
                first = sp + coefs[LEVELS + t, x, span, :] * r
                second = sr - coefs[t, x, span, :] * sp
                if shift:
                    first = first + shift * source[t, x, span, :]
                    second = second + shift * source[LEVELS + t, x, span, :]
                if final:
                    outs[k][t, x - DEPTH] = first
                    outs[k][LEVELS + t, x - DEPTH] = second
                else:
                    wm[t, x] = first
                    wm[LEVELS + t, x] = second

        if not final:
            @pl.loop(0, N)
            def _(x):
                for f in range(8):
                    outs[k][f, x] = wm[f, x + DEPTH, DEPTH : DEPTH + N, :]


def first_kernel(wide, upper, lower, select, inv, ginv, gcoefs, *refs):
    outs, scratch = refs[:DEPTH], refs[DEPTH:]
    place = [lax.axis_index("gx"), lax.axis_index("gy"), lax.axis_index(GZ)]
    lane = lax.broadcasted_iota(jnp.int32, (E, LANES), 1)
    row = lax.broadcasted_iota(jnp.int32, (E, LANES), 0)
    slot = lane // DEPTH

    def within(index, spot):
        return (index < E) & ((spot > 0) | (index >= DEPTH)) & ((spot < 3) | (index < DEPTH + N))

    y_in = within(row, place[1])
    ym = y_in.astype(F32)
    xy = (y_in & within(slot, place[0])).astype(F32)
    ends = ((place[2] < 7).astype(F32), (place[2] > 0).astype(F32))

    @pl.loop(0, E)
    def _(x):
        mask = ym * within(x, place[0]).astype(F32)
        for t in range(LEVELS):
            inv[t, x] = mask / (7.0 + wide[8 + t, x])

    for side, ghost in enumerate((upper, lower)):
        for t in range(LEVELS):
            ginv[side, t] = (xy * ends[side]) / (7.0 + ghost[8 + t])
            gcoefs[side, t] = ghost[12 + t]
            gcoefs[side, LEVELS + t] = ghost[16 + t]

    steps(SHIFT[:DEPTH], wide, (upper, lower), inv, wide.at[12:20], ginv, gcoefs, select, *scratch, outs)


def second_kernel(wide, upper, lower, select, inv, coefs, ginv, gcoefs, *refs):
    outs, scratch = refs[:DEPTH], refs[DEPTH:]
    steps(SHIFT[DEPTH:], wide, (upper, lower), inv, coefs.at[12:20], ginv, gcoefs, select, *scratch, outs)


def products(vectors, pairs):
    used = sorted({v for pair in pairs for v in pair})

    def add(i, sums):
        held = {v: vectors[v][i // N, i % N] for v in used}
        new = []
        for (a, b), total in zip(pairs, sums):
            product = held[a] * held[b]
            new.append(total + (product[:8] + product[8:]))
        return tuple(new)

    sums = lax.fori_loop(0, 8 * N, add, tuple(jnp.zeros((8, LANES), F32) for _ in pairs), unroll=4)
    return [jnp.sum(total, axis=0, keepdims=True) for total in sums]


def early_gram_kernel(*refs):
    vectors, out = refs[:-1], refs[-1]
    for n, row in enumerate(products(vectors, PAIRS[:EARLY])):
        out[n : n + 1, :] = row
    out[EARLY:, :] = jnp.zeros((1, LANES), F32)


def gram_kernel(early, *refs):
    vectors, out = refs[:-1], refs[-1]
    out[:EARLY, :] = early[:EARLY, :]
    for n, row in enumerate(products(vectors, PAIRS[EARLY:])):
        out[EARLY + n : EARLY + n + 1, :] = row
    out[len(PAIRS) :, :] = jnp.zeros((ROWS - len(PAIRS), LANES), F32)


def solve(gram):
    entry = {pair: gram[n : n + 1] for n, pair in enumerate(PAIRS)}
    upper = {}
    least = jnp.ones_like(entry[0, 0])
    for i in range(VECTORS):
        pivot = entry[i, i]
        for m in range(i):
            pivot = pivot - upper[m, i] * upper[m, i]
        least = jnp.minimum(least, pivot / entry[i, i])
        pivot = jnp.maximum(pivot, 1e-7 * entry[i, i])
        root = jnp.sqrt(pivot)
        upper[i, i] = root
        for j in range(i + 1, VECTORS):
            value = entry[i, j]
            for m in range(i):
                value = value - upper[m, i] * upper[m, j]
            upper[i, j] = value / root
    columns = []
    for c in range(ITERS):
        column = [(1.0 + SHIFT[c]) * upper[i, c] - upper[i, c + 1] for i in range(c + 1)]
        columns.append(column + [-upper[c + 1, c + 1]])
    return least, least_squares(columns, upper[0, 0], ITERS)


def least_squares(columns, beta, steps):
    rotations = []
    target = [beta] + [jnp.zeros_like(beta)] * steps
    upper = []
    for column_index in range(steps):
        column = list(columns[column_index])
        for place, (cosine, sine) in enumerate(rotations):
            upper_entry = cosine * column[place] + sine * column[place + 1]
            lower_entry = -sine * column[place] + cosine * column[place + 1]
            column[place], column[place + 1] = (upper_entry, lower_entry)
        radius = jnp.sqrt(column[column_index] ** 2 + column[column_index + 1] ** 2)
        cosine = column[column_index] / radius
        sine = column[column_index + 1] / radius
        column[column_index] = radius
        rotations.append((cosine, sine))
        target[column_index], target[column_index + 1] = (
            cosine * target[column_index],
            -sine * target[column_index],
        )
        upper.append(column[: column_index + 1])
    solved = [None] * steps
    for row_index in range(steps - 1, -1, -1):
        accum = target[row_index]
        for later_index in range(row_index + 1, steps):
            accum = accum - upper[later_index][row_index] * solved[later_index]
        solved[row_index] = accum / upper[row_index][row_index]
    return solved


def with_halo(shard, sides, width):
    edges = {}
    for axis, dim in sides:
        size, length = (lax.axis_size(axis), shard.shape[dim])
        up = [(i, (i + 1) % size) for i in range(size - 1)]
        last = lax.slice_in_dim(shard, length - width, length, axis=dim)
        first = lax.slice_in_dim(shard, 0, width, axis=dim)
        edges[dim] = (
            lax.ppermute(last, axis, up),
            lax.ppermute(first, axis, [(b, a) for a, b in up]),
        )
    done = []
    for _, dim in sides:
        low, high = edges[dim]
        around = [(width, width) if d in done else (0, 0) for d in range(shard.ndim)]
        shard = jnp.concatenate([jnp.pad(low, around), shard, jnp.pad(high, around)], axis=dim)
        done.append(dim)
    return shard


def stencil(padded):
    center = padded[..., 1:-1, 1:-1, 1:-1]
    beside = padded[..., 2:, 1:-1, 1:-1] + padded[..., :-2, 1:-1, 1:-1]
    beside = beside + padded[..., 1:-1, 2:, 1:-1] + padded[..., 1:-1, :-2, 1:-1]
    beside = beside + padded[..., 1:-1, 1:-1, 2:] + padded[..., 1:-1, 1:-1, :-2]
    return 6.0 * center - beside


def jacobian(vector, lapped, reaction, transport, congestion):
    value_part, density_part = (vector[0], vector[1])
    later = jnp.concatenate([value_part[1:], jnp.zeros_like(value_part[:1])], 0)
    earlier = jnp.concatenate([jnp.zeros_like(density_part[:1]), density_part[:-1]], 0)
    first = (
        (value_part - later)
        + lapped[0]
        + reaction * value_part
        - congestion * density_part
    )
    second = (
        (density_part - earlier)
        + lapped[1]
        + reaction * density_part
        - transport * lapped[0]
    )
    return jnp.stack([first, second], 0)


def precondition(vector, reaction, transport):
    levels = vector.shape[1]
    diag = 7.0 + reaction
    value_levels = [None] * levels
    carry = jnp.zeros_like(vector[0, 0])
    for level in range(levels - 1, -1, -1):
        carry = (vector[0, level] + carry) / diag[level]
        value_levels[level] = carry
    density_levels = []
    carry = jnp.zeros_like(vector[1, 0])
    for level in range(levels):
        carry = (
            vector[1, level] + carry + 6.0 * transport[level] * value_levels[level]
        ) / diag[level]
        density_levels.append(carry)
    return jnp.stack([jnp.stack(value_levels, 0), jnp.stack(density_levels, 0)], 0)


def lapped_field(search):
    padded = with_halo(search, (("gx", 2), ("gy", 3), (GZ, 4)), 1)
    return stencil(padded)


def careful(residual_in, reaction, transport, congestion):
    whole = lambda part: functools.reduce(lax.psum, GX_GY_GZ, part)
    spread = (slice(None),) + (None,) * residual_in.ndim
    beta = jnp.sqrt(whole(jnp.sum(residual_in * residual_in)))
    basis = jnp.zeros((VECTORS,) + residual_in.shape, F32).at[0].set(residual_in / beta)

    def column(c, state):
        basis, h = state
        search = precondition(lax.dynamic_index_in_dim(basis, c, 0, False), reaction, transport)
        image = jacobian(search, lapped_field(search), reaction, transport, congestion)
        coeffs = whole(jnp.sum(basis * image, axis=tuple(range(1, basis.ndim))))
        image = image - jnp.sum(coeffs[spread] * basis, axis=0)
        height = jnp.sqrt(whole(jnp.sum(image * image)))
        basis = lax.dynamic_update_index_in_dim(basis, image / height, c + 1, 0)
        coeffs = jnp.where(jnp.arange(VECTORS) == c + 1, height, coeffs)
        return basis, lax.dynamic_update_index_in_dim(h, coeffs, c, 0)

    basis, h = lax.fori_loop(0, ITERS, column, (basis, jnp.zeros((ITERS, VECTORS), F32)))
    columns = [[h[c, i] for i in range(c + 2)] for c in range(ITERS)]
    weights = jnp.stack(least_squares(columns, beta, ITERS))
    return precondition(jnp.sum(weights[spread] * basis[:ITERS], axis=0), reaction, transport)


def update_kernel(gram, rea, tra, *refs):
    vectors, (out, quality) = refs[:ITERS], refs[ITERS:]
    whole = jnp.broadcast_to(jnp.sum(gram[...], axis=1, keepdims=True), (ROWS, LANES))
    least, rows = solve(whole)
    quality[...] = jnp.broadcast_to(least, (8, LANES))
    weights = [jnp.broadcast_to(row, (N, LANES)) for row in rows]

    @pl.loop(0, N)
    def _(x):
        def mixed(f):
            total = weights[0] * vectors[0][f, x]
            for weight, vector in zip(weights[1:], vectors[1:]):
                total = total + weight * vector[f, x]
            return total

        inverse = [1.0 / (7.0 + rea[t, x]) for t in range(LEVELS)]
        p = [None] * LEVELS
        carry = None
        for t in range(LEVELS - 1, -1, -1):
            top = mixed(t)
            carry = (top if carry is None else top + carry) * inverse[t]
            p[t] = carry
            out[t, x] = carry
        carry = None
        for t in range(LEVELS):
            top = mixed(LEVELS + t) + 6.0 * tra[t, x] * p[t]
            carry = (top if carry is None else top + carry) * inverse[t]
            out[LEVELS + t, x] = carry


def exchange(slabs):
    received = []
    for slab, (dx, dy) in zip(slabs, WAYS):
        pairs = [(x * 4 + y, (x + dx) % 4 * 4 + (y + dy) % 4) for x in range(4) for y in range(4)]
        received.append(lax.ppermute(slab, ("gx", "gy"), pairs))
    return received


def exchange_z(low, high):
    from_above = lax.ppermute(low, GZ, [((i + 1) % 8, i) for i in range(8)])
    from_below = lax.ppermute(high, GZ, [(i, (i + 1) % 8) for i in range(8)])
    return from_above, from_below


def add_up(part):
    for axis in ("gz_1", "gx", "gy", "gz_0"):
        size = lax.axis_size(axis)
        got = [lax.ppermute(part, axis, [(i, i ^ d) for i in range(size)]) for d in range(1, size)]
        part = part + got[0] if size == 2 else (part + got[0]) + (got[1] + got[2])
    return part


def body(residual_in, reaction, transport, congestion):
    given = (residual_in.reshape(8, N, N, LANES), reaction, transport, congestion)
    given = [pltpu.with_memory_space_constraint(g, pltpu.HBM) for g in given]
    core, half, packed = (8, N, N, LANES), (4, N, N, LANES), (E, LANES)
    scratch = [vmem((8, E, E, LANES)), vmem((8, E, E + 2 * PAD, LANES)), vmem((2, 8) + packed)]
    scratch += [vmem((2, 8, E + 2 * PAD, LANES))]
    scratch += [vmem((8, E, E, LANES)), vmem((8,) + packed)]
    shape = lambda *s: jax.ShapeDtypeStruct(s, F32)

    def surround(slabs, held):
        fields = sum(h.shape[0] for h in held)
        received = exchange(slabs)
        inside = call(core_kernel, [vmem((fields, E, E, LANES))] + [vmem((fields, N, LANES))] * 2, *held)
        wide, low, high = call(
            widen_kernel,
            [vmem((fields, E, E, LANES)), shape(fields, *packed), shape(fields, *packed)],
            *inside, *received, alias={0: 0},
        )
        return wide, *exchange_z(low, high)

    *slabs, res, rea, tra, con = call(
        pack_kernel,
        [shape(*slab_shape(20, w)) for w in WAYS] + [vmem(core)] + [vmem(half)] * 3,
        *given, far=True, scratch=[pltpu.SemaphoreType.DMA((4,))],
    )
    select, = call(weights_kernel, [pltpu.VMEM((E, 2 * LANES, 2 * LANES), jnp.bfloat16)])
    fields, upper, lower = surround(slabs, (res, rea, tra, con))
    inv, ginv, gcoefs, *made = call(
        first_kernel,
        [vmem((4, E, E, LANES)), vmem((2, 4) + packed), vmem((2, 8) + packed)] + [vmem(core)] * DEPTH,
        fields, upper, lower, select, scratch=scratch,
    )
    slabs = call(slab_kernel, [shape(*slab_shape(8, w)) for w in WAYS], made[-1])
    early, = call(early_gram_kernel, [vmem((EARLY + 1, LANES))], res, *made)
    wide, upper, lower = surround(slabs, made[-1:])
    more = call(second_kernel, [vmem(core)] * DEPTH, wide, upper, lower, select, inv, fields, ginv, gcoefs, scratch=scratch)
    basis = [res] + list(made) + list(more)
    part, = call(gram_kernel, [shape(ROWS, LANES)], early, *basis)
    gram = add_up(part)
    out, quality = call(update_kernel, [shape(*core), shape(8, LANES)], gram, rea, tra, *basis[:ITERS])
    _, out = lax.while_loop(
        lambda state: jnp.logical_not(state[0] >= THIN),
        lambda state: (jnp.float32(1.0), careful(residual_in, reaction, transport, congestion)),
        (quality[0, 0], out.reshape(residual_in.shape)),
    )
    return out


def solution(mesh):
    torus = Mesh(
        mesh.devices.reshape(mesh.shape["gx"], mesh.shape["gy"], 4, 2), ("gx", "gy", "gz_0", "gz_1")
    )
    field = P(None, "gx", "gy", GZ)
    pair = P(None, None, "gx", "gy", GZ)
    return jax.shard_map(
        body, mesh=torus, in_specs=(pair, field, field, field), out_specs=pair, check_vma=False
    )
```

```python
import functools

import jax
import jax.numpy as jnp
from jax import lax
from jax.experimental import pallas as pl
from jax.experimental.pallas import tpu as pltpu
from jax.sharding import Mesh
from jax.sharding import PartitionSpec as P

ITERS = 8
LEVELS = 4
DEPTH = 4
N = 16
E = N + 2 * DEPTH
LANES = 128
PAD = 8
VECTORS = ITERS + 1
PAIRS = [(i, j) for j in range(VECTORS) for i in range(j + 1)]
EARLY = 15
ROWS = 48
GZ = ("gz_0", "gz_1")
GX_GY_GZ = ("gx", "gy", "gz_0", "gz_1")
THIN = 1e-3
SHIFT = (0.68, -0.68, 0.0, -0.392, 0.448, -0.57, 0.592, 0.208)
F32 = jnp.float32


def vmem(shape):
    return pltpu.VMEM(shape, F32)


def call(kernel, outs, *args, scratch=(), far=False, alias=None, cost=1000000):
    whole = pl.BlockSpec(memory_space=pltpu.VMEM)
    return pl.pallas_call(
        kernel,
        out_shape=outs,
        in_specs=[pl.BlockSpec(memory_space=pltpu.HBM) if far else whole] * len(args),
        out_specs=[pl.BlockSpec(memory_space=pltpu.SMEM) if out.shape == (1, 1) else whole for out in outs],
        scratch_shapes=list(scratch),
        input_output_aliases=alias or {},
        compiler_params=pltpu.CompilerParams(vmem_limit_bytes=LIMIT),
        cost_estimate=pl.CostEstimate(flops=cost, bytes_accessed=cost, transcendentals=0),
    )(*args)


LIMIT = 24 * 1024 * 1024
SLAB = {
    (-1, 0): (slice(0, DEPTH), slice(0, N)),
    (1, 0): (slice(N - DEPTH, N), slice(0, N)),
    (0, -1): (slice(0, N), slice(0, DEPTH)),
    (0, 1): (slice(0, N), slice(N - DEPTH, N)),
}
CORNERS = [(-1, -1), (1, 1), (-1, 1), (1, -1)]
STEPS_OUT = [(a, b) for a in range(1, DEPTH) for b in range(1, DEPTH) if a + b <= DEPTH]
WAYS = list(SLAB) + CORNERS


def landing(way):
    low = lambda d: DEPTH if d == 0 else (0 if d > 0 else DEPTH + N)
    size = lambda d: N if d == 0 else DEPTH
    return tuple(slice(low(d), low(d) + size(d)) for d in way)


def slab_shape(fields, way):
    if way in CORNERS:
        return (fields, len(STEPS_OUT), LANES)
    return (fields,) + tuple(N if d == 0 else DEPTH for d in way) + (LANES,)


def cut(core, f, outs, to):
    for out, way in zip(outs, WAYS):
        if way in SLAB:
            xs, ys = SLAB[way]
            out[to, :, :, :] = core[f, xs, ys, :]
        else:
            for n, (a, b) in enumerate(STEPS_OUT):
                x, y = (N - c if d > 0 else c - 1 for c, d in zip((a, b), way))
                out[to, n : n + 1, :] = core[f, x, y : y + 1, :]


def fill(wide, f, slabs):
    for slab, way in zip(slabs, WAYS):
        if way in SLAB:
            xs, ys = landing(way)
            wide[f, xs, ys, :] = slab[f]
        else:
            for n, (a, b) in enumerate(STEPS_OUT):
                x, y = (DEPTH - c if d > 0 else DEPTH + N + c - 1 for c, d in zip((a, b), way))
                wide[f, x, y : y + 1, :] = slab[f, n : n + 1, :]


def pack_kernel(res, rea, tra, con, *refs):
    slabs, held, done = refs[:8], refs[8:12], refs[12]
    copies = [pltpu.make_async_copy(src, dst, done.at[n]) for n, (src, dst) in enumerate(zip((res, rea, tra, con), held))]
    for copy in copies:
        copy.start()
    for copy, source, base in zip(copies, held, (0, 8, 12, 16)):
        copy.wait()

        @pl.loop(0, source.shape[0])
        def _(f):
            cut(source, f, slabs, base + f)


def slab_kernel(core, *outs):
    @pl.loop(0, 8)
    def _(f):
        cut(core, f, outs, f)


def pack_rows(rows, shape):
    slot = lax.broadcasted_iota(jnp.int32, shape, 1) // DEPTH
    lo = hi = jnp.zeros(shape, F32)
    for x, value in rows:
        rolled = pltpu.roll(value, DEPTH * x, 1) if x else value
        lo = jnp.where(slot == x, rolled, lo)
        hi = jnp.where(slot == (x - 1) % (LANES // DEPTH), rolled, hi)
    return lo, pltpu.roll(hi, DEPTH, 1)


def core_kernel(*refs):
    cores, (wide, low, high) = refs[:-3], refs[-3:]
    base = 0
    for core in cores:
        count = core.shape[0]

        @pl.loop(0, count)
        def _(f):
            for side in (0, DEPTH + N):
                wide[base + f, side : side + DEPTH] = jnp.zeros((DEPTH, E, LANES), F32)
            wide[base + f, DEPTH : DEPTH + N, DEPTH : DEPTH + N, :] = core[f]
            low[base + f], high[base + f] = pack_rows([(x + DEPTH, core[f, x]) for x in range(N)], (N, LANES))

        base = base + count


def widen_kernel(given, core_low, core_high, *refs):
    slabs, (wide, low, high) = refs[:8], refs[8:]
    slot = lax.broadcasted_iota(jnp.int32, (8, LANES), 1) // DEPTH
    row = lax.broadcasted_iota(jnp.int32, (8, LANES), 0)
    middle = (slot >= DEPTH) & (slot < DEPTH + N)
    tall = lax.broadcasted_iota(jnp.int32, (N, LANES), 1) // DEPTH
    tall = (tall >= DEPTH) & (tall < DEPTH + N)

    def widen(f):
        fill(wide, f, slabs)
        outside = [x for x in range(E) if not DEPTH <= x < DEPTH + N]
        sides = pack_rows([(x, wide[f, x]) for x in outside], (E, LANES))
        beyond = [
            (x, jnp.where(row < DEPTH, wide[f, x, 0:8, :], wide[f, x, E - 8 : E, :]))
            for x in range(DEPTH, DEPTH + N)
        ]
        ends = pack_rows(beyond, (8, LANES))
        for out, side, end, core in zip((low, high), sides, ends, (core_low, core_high)):
            out[f, 0:8, :] = jnp.where(middle & (row < DEPTH), end, side[0:8])
            out[f, 8 : E - 8, :] = side[8 : E - 8]
            out[f, E - 8 : E, :] = jnp.where(middle & (row >= 8 - DEPTH), end, side[E - 8 : E])
            span = slice(DEPTH, DEPTH + N)
            out[f, span, :] = jnp.where(tall, core[f], side[span])

    @pl.loop(0, wide.shape[0] // 2)
    def _(n):
        widen(2 * n)
        widen(2 * n + 1)


def weights_kernel(out):
    i = lax.broadcasted_iota(jnp.int32, (2 * LANES, 2 * LANES), 0)
    j = lax.broadcasted_iota(jnp.int32, (2 * LANES, 2 * LANES), 1)
    inside = (i < LANES) & (j < LANES) & ((i - j == 1) | (j - i == 1))

    @pl.loop(0, E)
    def _(x):
        slot = LANES + DEPTH * x
        above = ((i == LANES - 1) & (j == slot)) | ((i == slot) & (j == LANES - 1))
        below = ((i == 0) & (j == slot + 1)) | ((i == slot + 1) & (j == 0))
        out[x] = (inside | above | below).astype(F32).astype(jnp.bfloat16)


def halves(value):
    parts = []
    for _ in range(2):
        part = value.astype(jnp.bfloat16)
        parts.append(part)
        value = value - part.astype(F32)
    return parts


def steps(shifts, wide, ghosts, inv, coefs, ginv, gcoefs, select, wm, sm, gw, gs, along_z, ends, outs):
    lane = lax.broadcasted_iota(jnp.int32, (E, LANES), 1)
    place = lane % DEPTH
    wider = lax.broadcasted_iota(jnp.int32, (8 * E, LANES), 1)
    none = jnp.zeros((1, LANES), F32)

    @pl.loop(0, 8)
    def _(f):
        for x in range(E):
            sm[f, x, PAD - 1 : PAD, :] = none
            sm[f, x, PAD + E : PAD + E + 1, :] = none
        for side in range(2):
            gs[side, f, PAD - 1 : PAD, :] = none
            gs[side, f, PAD + E : PAD + E + 1, :] = none

    def precondition(w, v, transport, store):
        p = [None] * LEVELS
        carry = None
        for t in range(LEVELS - 1, -1, -1):
            top = w(t)
            carry = (top if carry is None else top + carry) * v(t)
            p[t] = carry
            store(t, carry)
        carry = None
        for t in range(LEVELS):
            top = w(LEVELS + t) + (6.0 * transport(t)) * p[t]
            carry = (top if carry is None else top + carry) * v(t)
            store(LEVELS + t, carry)

    middle = slice(PAD, PAD + E)
    for k, shift in enumerate(shifts):
        source = wide if k == 0 else wm
        beyond = [ghosts[side] if k == 0 else gw.at[side] for side in range(2)]
        final = k == len(shifts) - 1

        @pl.loop(k, E - k)
        def _(x):
            def store(f, value):
                sm[f, x, middle, :] = value

            precondition(lambda f: source[f, x], lambda t: inv[t, x], lambda t: coefs[t, x], store)

        for side in range(2):
            def store(f, value):
                gs[side, f, middle, :] = value

            precondition(lambda f: beyond[side][f], lambda t: ginv[side, t], lambda t: gcoefs[side, t], store)

        lower = pltpu.roll(gs[1, :, middle, :].reshape(8 * E, LANES), LANES - 2, 1)
        over = jnp.where(wider % DEPTH == 1, lower, gs[0, :, middle, :].reshape(8 * E, LANES))
        outer = jnp.concatenate(halves(over), axis=0)
        ends[...] = jnp.zeros_like(ends)

        group = (E - 2 * k - 2) // 2

        @pl.loop(0, 2)
        def _(n):
            packed = None
            for m in range(group):
                x = k + 1 + n * group + m
                parts = halves(sm[:, x, middle, :].reshape(8 * E, LANES))
                both = jnp.concatenate([jnp.concatenate(parts, axis=0), outer], axis=1)
                moved = jnp.dot(both, select[x], preferred_element_type=F32)
                rows = [moved[8 * E * i : 8 * E * (i + 1)] for i in range(len(parts))]
                total = functools.reduce(lambda a, b: a + b, rows)
                along_z[:, x] = total[:, :LANES].reshape(8, E, LANES)
                packed = total[:, LANES:] if packed is None else packed + total[:, LANES:]
            ends[...] += packed.reshape(8, E, LANES)

        def beside_ghost(f):
            inner = ends[f]
            sums = []
            for side in range(2):
                value = gs[side, f, middle, :]
                before, after = pltpu.roll(value, 1, 1), pltpu.roll(value, LANES - 1, 1)
                if side == 0:
                    before = jnp.where(place == 0, inner, before)
                else:
                    after = jnp.where(place == DEPTH - 1, pltpu.roll(inner, 2, 1), after)
                total = before + after + gs[side, f, PAD - 1 : PAD + E - 1, :] + gs[side, f, PAD + 1 : PAD + E + 1, :]
                sums.append(total + pltpu.roll(value, DEPTH, 1) + pltpu.roll(value, LANES - DEPTH, 1))
            return sums

        if not final:
            for t in range(LEVELS):
                p_sums, r_sums = beside_ghost(t), beside_ghost(LEVELS + t)
                for side in range(2):
                    first = p_sums[side] + gcoefs[side, LEVELS + t] * gs[side, LEVELS + t, middle, :]
                    second = r_sums[side] - gcoefs[side, t] * p_sums[side]
                    if shift:
                        first = first + shift * beyond[side][t]
                        second = second + shift * beyond[side][LEVELS + t]
                    gw[side, t] = first
                    gw[side, LEVELS + t] = second

        y0, rows = (DEPTH, N) if final else (0, E)
        span = slice(y0, y0 + rows)

        @pl.loop(k + 1, E - k - 1)
        def _(x):
            def around(f):
                across = sm[f, x - 1, PAD + y0 : PAD + y0 + rows, :] + sm[f, x + 1, PAD + y0 : PAD + y0 + rows, :]
                along = sm[f, x, PAD + y0 - 1 : PAD + y0 + rows - 1, :] + sm[f, x, PAD + y0 + 1 : PAD + y0 + rows + 1, :]
                return along_z[f, x, span, :] + (across + along)

            for t in range(LEVELS):
                sp, sr = around(t), around(LEVELS + t)
                r = sm[LEVELS + t, x, PAD + y0 : PAD + y0 + rows, :]
                first = sp + coefs[LEVELS + t, x, span, :] * r
                second = sr - coefs[t, x, span, :] * sp
                if shift:
                    first = first + shift * source[t, x, span, :]
                    second = second + shift * source[LEVELS + t, x, span, :]
                if final:
                    outs[k][t, x - DEPTH] = first
                    outs[k][LEVELS + t, x - DEPTH] = second
                else:
                    wm[t, x] = first
                    wm[LEVELS + t, x] = second

        if not final:
            @pl.loop(0, N)
            def _(x):
                for f in range(8):
                    outs[k][f, x] = wm[f, x + DEPTH, DEPTH : DEPTH + N, :]


def first_kernel(wide, upper, lower, select, inv, ginv, gcoefs, *refs):
    outs, scratch = refs[:DEPTH], refs[DEPTH:]
    place = [lax.axis_index("gx"), lax.axis_index("gy"), lax.axis_index(GZ)]
    lane = lax.broadcasted_iota(jnp.int32, (E, LANES), 1)
    row = lax.broadcasted_iota(jnp.int32, (E, LANES), 0)
    slot = lane // DEPTH

    def within(index, spot):
        return (index < E) & ((spot > 0) | (index >= DEPTH)) & ((spot < 3) | (index < DEPTH + N))

    y_in = within(row, place[1])
    ym = y_in.astype(F32)
    xy = (y_in & within(slot, place[0])).astype(F32)
    ends = ((place[2] < 7).astype(F32), (place[2] > 0).astype(F32))

    @pl.loop(0, E)
    def _(x):
        mask = ym * within(x, place[0]).astype(F32)
        for t in range(LEVELS):
            inv[t, x] = mask / (7.0 + wide[8 + t, x])

    for side, ghost in enumerate((upper, lower)):
        for t in range(LEVELS):
            ginv[side, t] = (xy * ends[side]) / (7.0 + ghost[8 + t])
            gcoefs[side, t] = ghost[12 + t]
            gcoefs[side, LEVELS + t] = ghost[16 + t]

    steps(SHIFT[:DEPTH], wide, (upper, lower), inv, wide.at[12:20], ginv, gcoefs, select, *scratch, outs)


def second_kernel(wide, upper, lower, select, inv, coefs, ginv, gcoefs, *refs):
    outs, scratch = refs[:DEPTH], refs[DEPTH:]
    steps(SHIFT[DEPTH:], wide, (upper, lower), inv, coefs.at[12:20], ginv, gcoefs, select, *scratch, outs)


def products(vectors, pairs):
    used = sorted({v for pair in pairs for v in pair})

    def add(i, sums):
        held = {v: vectors[v][i // N, i % N] for v in used}
        new = []
        for (a, b), total in zip(pairs, sums):
            product = held[a] * held[b]
            new.append(total + (product[:8] + product[8:]))
        return tuple(new)

    sums = lax.fori_loop(0, 8 * N, add, tuple(jnp.zeros((8, LANES), F32) for _ in pairs), unroll=4)
    return [jnp.sum(total, axis=0, keepdims=True) for total in sums]


def early_gram_kernel(*refs):
    vectors, out = refs[:-1], refs[-1]
    for n, row in enumerate(products(vectors, PAIRS[:EARLY])):
        out[n : n + 1, :] = row
    out[EARLY:, :] = jnp.zeros((1, LANES), F32)


def gram_kernel(early, *refs):
    vectors, out = refs[:-1], refs[-1]
    out[:EARLY, :] = early[:EARLY, :]
    for n, row in enumerate(products(vectors, PAIRS[EARLY:])):
        out[EARLY + n : EARLY + n + 1, :] = row
    out[len(PAIRS) :, :] = jnp.zeros((ROWS - len(PAIRS), LANES), F32)


def solve(gram):
    entry = {pair: gram[n : n + 1] for n, pair in enumerate(PAIRS)}
    upper = {}
    least = jnp.ones_like(entry[0, 0])
    for i in range(VECTORS):
        pivot = entry[i, i]
        for m in range(i):
            pivot = pivot - upper[m, i] * upper[m, i]
        least = jnp.minimum(least, pivot / entry[i, i])
        pivot = jnp.maximum(pivot, 1e-7 * entry[i, i])
        root = jnp.sqrt(pivot)
        upper[i, i] = root
        for j in range(i + 1, VECTORS):
            value = entry[i, j]
            for m in range(i):
                value = value - upper[m, i] * upper[m, j]
            upper[i, j] = value / root
    columns = []
    for c in range(ITERS):
        column = [(1.0 + SHIFT[c]) * upper[i, c] - upper[i, c + 1] for i in range(c + 1)]
        columns.append(column + [-upper[c + 1, c + 1]])
    return least, least_squares(columns, upper[0, 0], ITERS)


def least_squares(columns, beta, steps):
    rotations = []
    target = [beta] + [jnp.zeros_like(beta)] * steps
    upper = []
    for column_index in range(steps):
        column = list(columns[column_index])
        for place, (cosine, sine) in enumerate(rotations):
            upper_entry = cosine * column[place] + sine * column[place + 1]
            lower_entry = -sine * column[place] + cosine * column[place + 1]
            column[place], column[place + 1] = (upper_entry, lower_entry)
        radius = jnp.sqrt(column[column_index] ** 2 + column[column_index + 1] ** 2)
        cosine = column[column_index] / radius
        sine = column[column_index + 1] / radius
        column[column_index] = radius
        rotations.append((cosine, sine))
        target[column_index], target[column_index + 1] = (
            cosine * target[column_index],
            -sine * target[column_index],
        )
        upper.append(column[: column_index + 1])
    solved = [None] * steps
    for row_index in range(steps - 1, -1, -1):
        accum = target[row_index]
        for later_index in range(row_index + 1, steps):
            accum = accum - upper[later_index][row_index] * solved[later_index]
        solved[row_index] = accum / upper[row_index][row_index]
    return solved


def with_halo(shard, sides, width):
    edges = {}
    for axis, dim in sides:
        size, length = (lax.axis_size(axis), shard.shape[dim])
        up = [(i, (i + 1) % size) for i in range(size - 1)]
        last = lax.slice_in_dim(shard, length - width, length, axis=dim)
        first = lax.slice_in_dim(shard, 0, width, axis=dim)
        edges[dim] = (
            lax.ppermute(last, axis, up),
            lax.ppermute(first, axis, [(b, a) for a, b in up]),
        )
    done = []
    for _, dim in sides:
        low, high = edges[dim]
        around = [(width, width) if d in done else (0, 0) for d in range(shard.ndim)]
        shard = jnp.concatenate([jnp.pad(low, around), shard, jnp.pad(high, around)], axis=dim)
        done.append(dim)
    return shard


def stencil(padded):
    center = padded[..., 1:-1, 1:-1, 1:-1]
    beside = padded[..., 2:, 1:-1, 1:-1] + padded[..., :-2, 1:-1, 1:-1]
    beside = beside + padded[..., 1:-1, 2:, 1:-1] + padded[..., 1:-1, :-2, 1:-1]
    beside = beside + padded[..., 1:-1, 1:-1, 2:] + padded[..., 1:-1, 1:-1, :-2]
    return 6.0 * center - beside


def jacobian(vector, lapped, reaction, transport, congestion):
    value_part, density_part = (vector[0], vector[1])
    later = jnp.concatenate([value_part[1:], jnp.zeros_like(value_part[:1])], 0)
    earlier = jnp.concatenate([jnp.zeros_like(density_part[:1]), density_part[:-1]], 0)
    first = (
        (value_part - later)
        + lapped[0]
        + reaction * value_part
        - congestion * density_part
    )
    second = (
        (density_part - earlier)
        + lapped[1]
        + reaction * density_part
        - transport * lapped[0]
    )
    return jnp.stack([first, second], 0)


def precondition(vector, reaction, transport):
    levels = vector.shape[1]
    diag = 7.0 + reaction
    value_levels = [None] * levels
    carry = jnp.zeros_like(vector[0, 0])
    for level in range(levels - 1, -1, -1):
        carry = (vector[0, level] + carry) / diag[level]
        value_levels[level] = carry
    density_levels = []
    carry = jnp.zeros_like(vector[1, 0])
    for level in range(levels):
        carry = (
            vector[1, level] + carry + 6.0 * transport[level] * value_levels[level]
        ) / diag[level]
        density_levels.append(carry)
    return jnp.stack([jnp.stack(value_levels, 0), jnp.stack(density_levels, 0)], 0)


def lapped_field(search):
    padded = with_halo(search, (("gx", 2), ("gy", 3), (GZ, 4)), 1)
    return stencil(padded)


def careful(residual_in, reaction, transport, congestion):
    whole = lambda part: functools.reduce(lax.psum, GX_GY_GZ, part)
    spread = (slice(None),) + (None,) * residual_in.ndim
    beta = jnp.sqrt(whole(jnp.sum(residual_in * residual_in)))
    basis = jnp.zeros((VECTORS,) + residual_in.shape, F32).at[0].set(residual_in / beta)

    def column(c, state):
        basis, h = state
        search = precondition(lax.dynamic_index_in_dim(basis, c, 0, False), reaction, transport)
        image = jacobian(search, lapped_field(search), reaction, transport, congestion)
        coeffs = whole(jnp.sum(basis * image, axis=tuple(range(1, basis.ndim))))
        image = image - jnp.sum(coeffs[spread] * basis, axis=0)
        height = jnp.sqrt(whole(jnp.sum(image * image)))
        basis = lax.dynamic_update_index_in_dim(basis, image / height, c + 1, 0)
        coeffs = jnp.where(jnp.arange(VECTORS) == c + 1, height, coeffs)
        return basis, lax.dynamic_update_index_in_dim(h, coeffs, c, 0)

    basis, h = lax.fori_loop(0, ITERS, column, (basis, jnp.zeros((ITERS, VECTORS), F32)))
    columns = [[h[c, i] for i in range(c + 2)] for c in range(ITERS)]
    weights = jnp.stack(least_squares(columns, beta, ITERS))
    return precondition(jnp.sum(weights[spread] * basis[:ITERS], axis=0), reaction, transport)


def update_kernel(gram, rea, tra, *refs):
    vectors, (out, quality) = refs[:ITERS], refs[ITERS:]
    whole = jnp.broadcast_to(jnp.sum(gram[...], axis=1, keepdims=True), (ROWS, LANES))
    least, rows = solve(whole)
    quality[0, 0] = least[0, 0]
    weights = [jnp.broadcast_to(row, (N, LANES)) for row in rows]

    @pl.loop(0, N)
    def _(x):
        def mixed(f):
            total = weights[0] * vectors[0][f, x]
            for weight, vector in zip(weights[1:], vectors[1:]):
                total = total + weight * vector[f, x]
            return total

        inverse = [1.0 / (7.0 + rea[t, x]) for t in range(LEVELS)]
        p = [None] * LEVELS
        carry = None
        for t in range(LEVELS - 1, -1, -1):
            top = mixed(t)
            carry = (top if carry is None else top + carry) * inverse[t]
            p[t] = carry
            out[t, x] = carry
        carry = None
        for t in range(LEVELS):
            top = mixed(LEVELS + t) + 6.0 * tra[t, x] * p[t]
            carry = (top if carry is None else top + carry) * inverse[t]
            out[LEVELS + t, x] = carry


def exchange(slabs):
    received = []
    for slab, (dx, dy) in zip(slabs, WAYS):
        pairs = [(x * 4 + y, (x + dx) % 4 * 4 + (y + dy) % 4) for x in range(4) for y in range(4)]
        received.append(lax.ppermute(slab, ("gx", "gy"), pairs))
    return received


def exchange_z(low, high):
    from_above = lax.ppermute(low, GZ, [((i + 1) % 8, i) for i in range(8)])
    from_below = lax.ppermute(high, GZ, [(i, (i + 1) % 8) for i in range(8)])
    return from_above, from_below


def add_up(part):
    for axis in ("gz_1", "gx", "gy", "gz_0"):
        size = lax.axis_size(axis)
        got = [lax.ppermute(part, axis, [(i, i ^ d) for i in range(size)]) for d in range(1, size)]
        part = part + got[0] if size == 2 else (part + got[0]) + (got[1] + got[2])
    return part


def body(residual_in, reaction, transport, congestion):
    given = (residual_in.reshape(8, N, N, LANES), reaction, transport, congestion)
    given = [pltpu.with_memory_space_constraint(g, pltpu.HBM) for g in given]
    core, half, packed = (8, N, N, LANES), (4, N, N, LANES), (E, LANES)
    scratch = [vmem((8, E, E, LANES)), vmem((8, E, E + 2 * PAD, LANES)), vmem((2, 8) + packed)]
    scratch += [vmem((2, 8, E + 2 * PAD, LANES))]
    scratch += [vmem((8, E, E, LANES)), vmem((8,) + packed)]
    shape = lambda *s: jax.ShapeDtypeStruct(s, F32)

    def surround(slabs, held):
        fields = sum(h.shape[0] for h in held)
        received = exchange(slabs)
        inside = call(core_kernel, [vmem((fields, E, E, LANES))] + [vmem((fields, N, LANES))] * 2, *held)
        wide, low, high = call(
            widen_kernel,
            [vmem((fields, E, E, LANES)), shape(fields, *packed), shape(fields, *packed)],
            *inside, *received, alias={0: 0},
        )
        return wide, *exchange_z(low, high)

    *slabs, res, rea, tra, con = call(
        pack_kernel,
        [shape(*slab_shape(20, w)) for w in WAYS] + [vmem(core)] + [vmem(half)] * 3,
        *given, far=True, scratch=[pltpu.SemaphoreType.DMA((4,))],
    )
    select, = call(weights_kernel, [pltpu.VMEM((E, 2 * LANES, 2 * LANES), jnp.bfloat16)])
    fields, upper, lower = surround(slabs, (res, rea, tra, con))
    inv, ginv, gcoefs, *made = call(
        first_kernel,
        [vmem((4, E, E, LANES)), vmem((2, 4) + packed), vmem((2, 8) + packed)] + [vmem(core)] * DEPTH,
        fields, upper, lower, select, scratch=scratch,
    )
    slabs = call(slab_kernel, [shape(*slab_shape(8, w)) for w in WAYS], made[-1])
    early, = call(early_gram_kernel, [vmem((EARLY + 1, LANES))], res, *made)
    wide, upper, lower = surround(slabs, made[-1:])
    more = call(second_kernel, [vmem(core)] * DEPTH, wide, upper, lower, select, inv, fields, ginv, gcoefs, scratch=scratch)
    basis = [res] + list(made) + list(more)
    part, = call(gram_kernel, [shape(ROWS, LANES)], early, *basis)
    gram = add_up(part)
    out, quality = call(update_kernel, [shape(*core), shape(1, 1)], gram, rea, tra, *basis[:ITERS])
    _, out = lax.while_loop(
        lambda state: jnp.logical_not(state[0] >= THIN),
        lambda state: (jnp.float32(1.0), careful(residual_in, reaction, transport, congestion)),
        (quality[0, 0], out.reshape(residual_in.shape)),
    )
    return out


def solution(mesh):
    torus = Mesh(
        mesh.devices.reshape(mesh.shape["gx"], mesh.shape["gy"], 4, 2), ("gx", "gy", "gz_0", "gz_1")
    )
    field = P(None, "gx", "gy", GZ)
    pair = P(None, None, "gx", "gy", GZ)
    return jax.shard_map(
        body, mesh=torus, in_specs=(pair, field, field, field), out_specs=pair, check_vma=False
    )
```

```python
import functools

import jax
import jax.numpy as jnp
from jax import lax
from jax.experimental import pallas as pl
from jax.experimental.pallas import tpu as pltpu
from jax.sharding import Mesh
from jax.sharding import PartitionSpec as P

ITERS = 8
LEVELS = 4
DEPTH = 4
N = 16
E = N + 2 * DEPTH
LANES = 128
PAD = 8
VECTORS = ITERS + 1
PAIRS = [(i, j) for j in range(VECTORS) for i in range(j + 1)]
EARLY = 15
ROWS = 48
GZ = ("gz_0", "gz_1")
GX_GY_GZ = ("gx", "gy", "gz_0", "gz_1")
THIN = 1e-3
SHIFT = (0.68, -0.68, 0.0, -0.392, 0.448, -0.57, 0.592, 0.208)
F32 = jnp.float32


def vmem(shape):
    return pltpu.VMEM(shape, F32)


def call(kernel, outs, *args, scratch=(), far=False, alias=None, cost=1000000):
    whole = pl.BlockSpec(memory_space=pltpu.VMEM)
    return pl.pallas_call(
        kernel,
        out_shape=outs,
        in_specs=[pl.BlockSpec(memory_space=pltpu.HBM) if far else whole] * len(args),
        out_specs=[pl.BlockSpec(memory_space=pltpu.SMEM) if out.shape == (1, 1) else whole for out in outs],
        scratch_shapes=list(scratch),
        input_output_aliases=alias or {},
        compiler_params=pltpu.CompilerParams(vmem_limit_bytes=LIMIT),
        cost_estimate=pl.CostEstimate(flops=cost, bytes_accessed=cost, transcendentals=0),
    )(*args)


LIMIT = 24 * 1024 * 1024
SLAB = {
    (-1, 0): (slice(0, DEPTH), slice(0, N)),
    (1, 0): (slice(N - DEPTH, N), slice(0, N)),
    (0, -1): (slice(0, N), slice(0, DEPTH)),
    (0, 1): (slice(0, N), slice(N - DEPTH, N)),
}
CORNERS = [(-1, -1), (1, 1), (-1, 1), (1, -1)]
STEPS_OUT = [(a, b) for a in range(1, DEPTH) for b in range(1, DEPTH) if a + b <= DEPTH]
WAYS = list(SLAB) + CORNERS


def landing(way):
    low = lambda d: DEPTH if d == 0 else (0 if d > 0 else DEPTH + N)
    size = lambda d: N if d == 0 else DEPTH
    return tuple(slice(low(d), low(d) + size(d)) for d in way)


def slab_shape(fields, way):
    if way in CORNERS:
        return (fields, len(STEPS_OUT), LANES)
    return (fields,) + tuple(N if d == 0 else DEPTH for d in way) + (LANES,)


def cut(core, f, outs, to):
    for out, way in zip(outs, WAYS):
        if way in SLAB:
            xs, ys = SLAB[way]
            out[to, :, :, :] = core[f, xs, ys, :]
        else:
            for n, (a, b) in enumerate(STEPS_OUT):
                x, y = (N - c if d > 0 else c - 1 for c, d in zip((a, b), way))
                out[to, n : n + 1, :] = core[f, x, y : y + 1, :]


def fill(wide, f, slabs):
    for slab, way in zip(slabs, WAYS):
        if way in SLAB:
            xs, ys = landing(way)
            wide[f, xs, ys, :] = slab[f]
        else:
            for n, (a, b) in enumerate(STEPS_OUT):
                x, y = (DEPTH - c if d > 0 else DEPTH + N + c - 1 for c, d in zip((a, b), way))
                wide[f, x, y : y + 1, :] = slab[f, n : n + 1, :]


def pack_kernel(res, rea, tra, con, *refs):
    slabs, held, done = refs[:8], refs[8:12], refs[12]
    copies = [pltpu.make_async_copy(src, dst, done.at[n]) for n, (src, dst) in enumerate(zip((res, rea, tra, con), held))]
    for copy in copies:
        copy.start()
    for copy, source, base in zip(copies, held, (0, 8, 12, 16)):
        copy.wait()

        @pl.loop(0, source.shape[0])
        def _(f):
            cut(source, f, slabs, base + f)


def slab_kernel(core, *outs):
    @pl.loop(0, 8)
    def _(f):
        cut(core, f, outs, f)


def pack_rows(rows, shape):
    slot = lax.broadcasted_iota(jnp.int32, shape, 1) // DEPTH
    lo = hi = jnp.zeros(shape, F32)
    for x, value in rows:
        rolled = pltpu.roll(value, DEPTH * x, 1) if x else value
        lo = jnp.where(slot == x, rolled, lo)
        hi = jnp.where(slot == (x - 1) % (LANES // DEPTH), rolled, hi)
    return lo, pltpu.roll(hi, DEPTH, 1)


def core_kernel(*refs):
    cores, (wide, low, high) = refs[:-3], refs[-3:]
    base = 0
    for core in cores:
        count = core.shape[0]

        @pl.loop(0, count)
        def _(f):
            for side in (0, DEPTH + N):
                wide[base + f, side : side + DEPTH] = jnp.zeros((DEPTH, E, LANES), F32)
            wide[base + f, DEPTH : DEPTH + N, DEPTH : DEPTH + N, :] = core[f]
            low[base + f], high[base + f] = pack_rows([(x + DEPTH, core[f, x]) for x in range(N)], (N, LANES))

        base = base + count


def widen_kernel(given, core_low, core_high, *refs):
    slabs, (wide, low, high) = refs[:8], refs[8:]
    slot = lax.broadcasted_iota(jnp.int32, (8, LANES), 1) // DEPTH
    row = lax.broadcasted_iota(jnp.int32, (8, LANES), 0)
    middle = (slot >= DEPTH) & (slot < DEPTH + N)
    tall = lax.broadcasted_iota(jnp.int32, (N, LANES), 1) // DEPTH
    tall = (tall >= DEPTH) & (tall < DEPTH + N)

    def widen(f):
        fill(wide, f, slabs)
        outside = [x for x in range(E) if not DEPTH <= x < DEPTH + N]
        sides = pack_rows([(x, wide[f, x]) for x in outside], (E, LANES))
        beyond = [
            (x, jnp.where(row < DEPTH, wide[f, x, 0:8, :], wide[f, x, E - 8 : E, :]))
            for x in range(DEPTH, DEPTH + N)
        ]
        ends = pack_rows(beyond, (8, LANES))
        for out, side, end, core in zip((low, high), sides, ends, (core_low, core_high)):
            out[f, 0:8, :] = jnp.where(middle & (row < DEPTH), end, side[0:8])
            out[f, 8 : E - 8, :] = side[8 : E - 8]
            out[f, E - 8 : E, :] = jnp.where(middle & (row >= 8 - DEPTH), end, side[E - 8 : E])
            span = slice(DEPTH, DEPTH + N)
            out[f, span, :] = jnp.where(tall, core[f], side[span])

    @pl.loop(0, wide.shape[0] // 2)
    def _(n):
        widen(2 * n)
        widen(2 * n + 1)


def weights_kernel(out):
    i = lax.broadcasted_iota(jnp.int32, (2 * LANES, 2 * LANES), 0)
    j = lax.broadcasted_iota(jnp.int32, (2 * LANES, 2 * LANES), 1)
    inside = (i < LANES) & (j < LANES) & ((i - j == 1) | (j - i == 1))

    @pl.loop(0, E)
    def _(x):
        slot = LANES + DEPTH * x
        above = ((i == LANES - 1) & (j == slot)) | ((i == slot) & (j == LANES - 1))
        below = ((i == 0) & (j == slot + 1)) | ((i == slot + 1) & (j == 0))
        out[x] = (inside | above | below).astype(F32).astype(jnp.bfloat16)


def halves(value):
    parts = []
    for _ in range(2):
        part = value.astype(jnp.bfloat16)
        parts.append(part)
        value = value - part.astype(F32)
    return parts


def steps(shifts, wide, ghosts, inv, coefs, ginv, gcoefs, select, wm, sm, gw, gs, along_z, ends, outs):
    lane = lax.broadcasted_iota(jnp.int32, (E, LANES), 1)
    place = lane % DEPTH
    wider = lax.broadcasted_iota(jnp.int32, (8 * E, LANES), 1)
    none = jnp.zeros((1, LANES), F32)

    @pl.loop(0, 8)
    def _(f):
        for x in range(E):
            sm[f, x, PAD - 1 : PAD, :] = none
            sm[f, x, PAD + E : PAD + E + 1, :] = none
        for side in range(2):
            gs[side, f, PAD - 1 : PAD, :] = none
            gs[side, f, PAD + E : PAD + E + 1, :] = none

    def precondition(w, v, transport, store):
        p = [None] * LEVELS
        carry = None
        for t in range(LEVELS - 1, -1, -1):
            top = w(t)
            carry = (top if carry is None else top + carry) * v(t)
            p[t] = carry
            store(t, carry)
        carry = None
        for t in range(LEVELS):
            top = w(LEVELS + t) + (6.0 * transport(t)) * p[t]
            carry = (top if carry is None else top + carry) * v(t)
            store(LEVELS + t, carry)

    middle = slice(PAD, PAD + E)
    for k, shift in enumerate(shifts):
        source = wide if k == 0 else wm
        beyond = [ghosts[side] if k == 0 else gw.at[side] for side in range(2)]
        final = k == len(shifts) - 1

        @pl.loop(k, E - k, unroll=2)
        def _(x):
            def store(f, value):
                sm[f, x, middle, :] = value

            precondition(lambda f: source[f, x], lambda t: inv[t, x], lambda t: coefs[t, x], store)

        for side in range(2):
            def store(f, value):
                gs[side, f, middle, :] = value

            precondition(lambda f: beyond[side][f], lambda t: ginv[side, t], lambda t: gcoefs[side, t], store)

        y0, rows = (DEPTH, N) if final else (0, E)
        span = slice(y0, y0 + rows)
        here = slice(PAD + y0, PAD + y0 + rows)
        upper, lower = (gs[side, :, here, :].reshape(8 * rows, LANES) for side in range(2))
        over = jnp.where(wider[: 8 * rows] % DEPTH == 1, pltpu.roll(lower, LANES - 2, 1), upper)
        outer = jnp.concatenate(halves(over), axis=0)
        packed = None
        for x in range(k + 1, E - k - 1):
            parts = halves(sm[:, x, here, :].reshape(8 * rows, LANES))
            both = jnp.concatenate([jnp.concatenate(parts, axis=0), outer], axis=1)
            matrix = select[x, :, :LANES] if final else select[x]
            moved = jnp.dot(both, matrix, preferred_element_type=F32)
            total = moved[: 8 * rows] + moved[8 * rows :]
            along_z[:, x, :rows, :] = total[:, :LANES].reshape(8, rows, LANES)
            if not final:
                packed = total[:, LANES:] if packed is None else packed + total[:, LANES:]
        if not final:
            ends[...] = packed.reshape(8, E, LANES)

        def beside_ghost(f):
            inner = ends[f]
            sums = []
            for side in range(2):
                value = gs[side, f, middle, :]
                before, after = pltpu.roll(value, 1, 1), pltpu.roll(value, LANES - 1, 1)
                if side == 0:
                    before = jnp.where(place == 0, inner, before)
                else:
                    after = jnp.where(place == DEPTH - 1, pltpu.roll(inner, 2, 1), after)
                total = before + after + gs[side, f, PAD - 1 : PAD + E - 1, :] + gs[side, f, PAD + 1 : PAD + E + 1, :]
                sums.append(total + pltpu.roll(value, DEPTH, 1) + pltpu.roll(value, LANES - DEPTH, 1))
            return sums

        if not final:
            for t in range(LEVELS):
                p_sums, r_sums = beside_ghost(t), beside_ghost(LEVELS + t)
                for side in range(2):
                    first = p_sums[side] + gcoefs[side, LEVELS + t] * gs[side, LEVELS + t, middle, :]
                    second = r_sums[side] - gcoefs[side, t] * p_sums[side]
                    if shift:
                        first = first + shift * beyond[side][t]
                        second = second + shift * beyond[side][LEVELS + t]
                    gw[side, t] = first
                    gw[side, LEVELS + t] = second

        @pl.loop(k + 1, E - k - 1, unroll=2)
        def _(x):
            def around(f):
                across = sm[f, x - 1, PAD + y0 : PAD + y0 + rows, :] + sm[f, x + 1, PAD + y0 : PAD + y0 + rows, :]
                along = sm[f, x, PAD + y0 - 1 : PAD + y0 + rows - 1, :] + sm[f, x, PAD + y0 + 1 : PAD + y0 + rows + 1, :]
                return along_z[f, x, :rows, :] + (across + along)

            for t in range(LEVELS):
                sp, sr = around(t), around(LEVELS + t)
                r = sm[LEVELS + t, x, PAD + y0 : PAD + y0 + rows, :]
                first = sp + coefs[LEVELS + t, x, span, :] * r
                second = sr - coefs[t, x, span, :] * sp
                if shift:
                    first = first + shift * source[t, x, span, :]
                    second = second + shift * source[LEVELS + t, x, span, :]
                if final:
                    outs[k][t, x - DEPTH] = first
                    outs[k][LEVELS + t, x - DEPTH] = second
                else:
                    wm[t, x] = first
                    wm[LEVELS + t, x] = second

        if not final:
            @pl.loop(0, N)
            def _(x):
                for f in range(8):
                    outs[k][f, x] = wm[f, x + DEPTH, DEPTH : DEPTH + N, :]


def first_kernel(wide, upper, lower, select, inv, ginv, gcoefs, *refs):
    outs, scratch = refs[:DEPTH], refs[DEPTH:]
    place = [lax.axis_index("gx"), lax.axis_index("gy"), lax.axis_index(GZ)]
    lane = lax.broadcasted_iota(jnp.int32, (E, LANES), 1)
    row = lax.broadcasted_iota(jnp.int32, (E, LANES), 0)
    slot = lane // DEPTH

    def within(index, spot):
        return (index < E) & ((spot > 0) | (index >= DEPTH)) & ((spot < 3) | (index < DEPTH + N))

    y_in = within(row, place[1])
    ym = y_in.astype(F32)
    xy = (y_in & within(slot, place[0])).astype(F32)
    ends = ((place[2] < 7).astype(F32), (place[2] > 0).astype(F32))

    @pl.loop(0, E)
    def _(x):
        mask = ym * within(x, place[0]).astype(F32)
        for t in range(LEVELS):
            inv[t, x] = mask / (7.0 + wide[8 + t, x])

    for side, ghost in enumerate((upper, lower)):
        for t in range(LEVELS):
            ginv[side, t] = (xy * ends[side]) / (7.0 + ghost[8 + t])
            gcoefs[side, t] = ghost[12 + t]
            gcoefs[side, LEVELS + t] = ghost[16 + t]

    steps(SHIFT[:DEPTH], wide, (upper, lower), inv, wide.at[12:20], ginv, gcoefs, select, *scratch, outs)


def second_kernel(wide, upper, lower, select, inv, coefs, ginv, gcoefs, *refs):
    outs, scratch = refs[:DEPTH], refs[DEPTH:]
    steps(SHIFT[DEPTH:], wide, (upper, lower), inv, coefs.at[12:20], ginv, gcoefs, select, *scratch, outs)


def products(vectors, pairs):
    used = sorted({v for pair in pairs for v in pair})

    def add(i, sums):
        held = {v: vectors[v][i // N, i % N] for v in used}
        new = []
        for (a, b), total in zip(pairs, sums):
            product = held[a] * held[b]
            new.append(total + (product[:8] + product[8:]))
        return tuple(new)

    sums = lax.fori_loop(0, 8 * N, add, tuple(jnp.zeros((8, LANES), F32) for _ in pairs), unroll=4)
    return [jnp.sum(total, axis=0, keepdims=True) for total in sums]


def early_gram_kernel(*refs):
    vectors, out = refs[:-1], refs[-1]
    for n, row in enumerate(products(vectors, PAIRS[:EARLY])):
        out[n : n + 1, :] = row
    out[EARLY:, :] = jnp.zeros((1, LANES), F32)


def gram_kernel(early, *refs):
    vectors, out = refs[:-1], refs[-1]
    out[:EARLY, :] = early[:EARLY, :]
    for n, row in enumerate(products(vectors, PAIRS[EARLY:])):
        out[EARLY + n : EARLY + n + 1, :] = row
    out[len(PAIRS) :, :] = jnp.zeros((ROWS - len(PAIRS), LANES), F32)


def solve(gram):
    entry = {pair: gram[n : n + 1] for n, pair in enumerate(PAIRS)}
    upper = {}
    least = jnp.ones_like(entry[0, 0])
    for i in range(VECTORS):
        pivot = entry[i, i]
        for m in range(i):
            pivot = pivot - upper[m, i] * upper[m, i]
        least = jnp.minimum(least, pivot / entry[i, i])
        pivot = jnp.maximum(pivot, 1e-7 * entry[i, i])
        root = jnp.sqrt(pivot)
        upper[i, i] = root
        for j in range(i + 1, VECTORS):
            value = entry[i, j]
            for m in range(i):
                value = value - upper[m, i] * upper[m, j]
            upper[i, j] = value / root
    columns = []
    for c in range(ITERS):
        column = [(1.0 + SHIFT[c]) * upper[i, c] - upper[i, c + 1] for i in range(c + 1)]
        columns.append(column + [-upper[c + 1, c + 1]])
    return least, least_squares(columns, upper[0, 0], ITERS)


def least_squares(columns, beta, steps):
    rotations = []
    target = [beta] + [jnp.zeros_like(beta)] * steps
    upper = []
    for column_index in range(steps):
        column = list(columns[column_index])
        for place, (cosine, sine) in enumerate(rotations):
            upper_entry = cosine * column[place] + sine * column[place + 1]
            lower_entry = -sine * column[place] + cosine * column[place + 1]
            column[place], column[place + 1] = (upper_entry, lower_entry)
        radius = jnp.sqrt(column[column_index] ** 2 + column[column_index + 1] ** 2)
        cosine = column[column_index] / radius
        sine = column[column_index + 1] / radius
        column[column_index] = radius
        rotations.append((cosine, sine))
        target[column_index], target[column_index + 1] = (
            cosine * target[column_index],
            -sine * target[column_index],
        )
        upper.append(column[: column_index + 1])
    solved = [None] * steps
    for row_index in range(steps - 1, -1, -1):
        accum = target[row_index]
        for later_index in range(row_index + 1, steps):
            accum = accum - upper[later_index][row_index] * solved[later_index]
        solved[row_index] = accum / upper[row_index][row_index]
    return solved


def with_halo(shard, sides, width):
    edges = {}
    for axis, dim in sides:
        size, length = (lax.axis_size(axis), shard.shape[dim])
        up = [(i, (i + 1) % size) for i in range(size - 1)]
        last = lax.slice_in_dim(shard, length - width, length, axis=dim)
        first = lax.slice_in_dim(shard, 0, width, axis=dim)
        edges[dim] = (
            lax.ppermute(last, axis, up),
            lax.ppermute(first, axis, [(b, a) for a, b in up]),
        )
    done = []
    for _, dim in sides:
        low, high = edges[dim]
        around = [(width, width) if d in done else (0, 0) for d in range(shard.ndim)]
        shard = jnp.concatenate([jnp.pad(low, around), shard, jnp.pad(high, around)], axis=dim)
        done.append(dim)
    return shard


def stencil(padded):
    center = padded[..., 1:-1, 1:-1, 1:-1]
    beside = padded[..., 2:, 1:-1, 1:-1] + padded[..., :-2, 1:-1, 1:-1]
    beside = beside + padded[..., 1:-1, 2:, 1:-1] + padded[..., 1:-1, :-2, 1:-1]
    beside = beside + padded[..., 1:-1, 1:-1, 2:] + padded[..., 1:-1, 1:-1, :-2]
    return 6.0 * center - beside


def jacobian(vector, lapped, reaction, transport, congestion):
    value_part, density_part = (vector[0], vector[1])
    later = jnp.concatenate([value_part[1:], jnp.zeros_like(value_part[:1])], 0)
    earlier = jnp.concatenate([jnp.zeros_like(density_part[:1]), density_part[:-1]], 0)
    first = (
        (value_part - later)
        + lapped[0]
        + reaction * value_part
        - congestion * density_part
    )
    second = (
        (density_part - earlier)
        + lapped[1]
        + reaction * density_part
        - transport * lapped[0]
    )
    return jnp.stack([first, second], 0)


def precondition(vector, reaction, transport):
    levels = vector.shape[1]
    diag = 7.0 + reaction
    value_levels = [None] * levels
    carry = jnp.zeros_like(vector[0, 0])
    for level in range(levels - 1, -1, -1):
        carry = (vector[0, level] + carry) / diag[level]
        value_levels[level] = carry
    density_levels = []
    carry = jnp.zeros_like(vector[1, 0])
    for level in range(levels):
        carry = (
            vector[1, level] + carry + 6.0 * transport[level] * value_levels[level]
        ) / diag[level]
        density_levels.append(carry)
    return jnp.stack([jnp.stack(value_levels, 0), jnp.stack(density_levels, 0)], 0)


def lapped_field(search):
    padded = with_halo(search, (("gx", 2), ("gy", 3), (GZ, 4)), 1)
    return stencil(padded)


def careful(residual_in, reaction, transport, congestion):
    whole = lambda part: functools.reduce(lax.psum, GX_GY_GZ, part)
    spread = (slice(None),) + (None,) * residual_in.ndim
    beta = jnp.sqrt(whole(jnp.sum(residual_in * residual_in)))
    basis = jnp.zeros((VECTORS,) + residual_in.shape, F32).at[0].set(residual_in / beta)

    def column(c, state):
        basis, h = state
        search = precondition(lax.dynamic_index_in_dim(basis, c, 0, False), reaction, transport)
        image = jacobian(search, lapped_field(search), reaction, transport, congestion)
        coeffs = whole(jnp.sum(basis * image, axis=tuple(range(1, basis.ndim))))
        image = image - jnp.sum(coeffs[spread] * basis, axis=0)
        height = jnp.sqrt(whole(jnp.sum(image * image)))
        basis = lax.dynamic_update_index_in_dim(basis, image / height, c + 1, 0)
        coeffs = jnp.where(jnp.arange(VECTORS) == c + 1, height, coeffs)
        return basis, lax.dynamic_update_index_in_dim(h, coeffs, c, 0)

    basis, h = lax.fori_loop(0, ITERS, column, (basis, jnp.zeros((ITERS, VECTORS), F32)))
    columns = [[h[c, i] for i in range(c + 2)] for c in range(ITERS)]
    weights = jnp.stack(least_squares(columns, beta, ITERS))
    return precondition(jnp.sum(weights[spread] * basis[:ITERS], axis=0), reaction, transport)


def update_kernel(gram, rea, tra, *refs):
    vectors, (out, quality) = refs[:ITERS], refs[ITERS:]
    whole = jnp.broadcast_to(jnp.sum(gram[...], axis=1, keepdims=True), (ROWS, LANES))
    least, rows = solve(whole)
    quality[0, 0] = least[0, 0]
    weights = [jnp.broadcast_to(row, (N, LANES)) for row in rows]

    @pl.loop(0, N)
    def _(x):
        def mixed(f):
            total = weights[0] * vectors[0][f, x]
            for weight, vector in zip(weights[1:], vectors[1:]):
                total = total + weight * vector[f, x]
            return total

        inverse = [1.0 / (7.0 + rea[t, x]) for t in range(LEVELS)]
        p = [None] * LEVELS
        carry = None
        for t in range(LEVELS - 1, -1, -1):
            top = mixed(t)
            carry = (top if carry is None else top + carry) * inverse[t]
            p[t] = carry
            out[t, x] = carry
        carry = None
        for t in range(LEVELS):
            top = mixed(LEVELS + t) + 6.0 * tra[t, x] * p[t]
            carry = (top if carry is None else top + carry) * inverse[t]
            out[LEVELS + t, x] = carry


def exchange(slabs):
    received = []
    for slab, (dx, dy) in zip(slabs, WAYS):
        pairs = [(x * 4 + y, (x + dx) % 4 * 4 + (y + dy) % 4) for x in range(4) for y in range(4)]
        received.append(lax.ppermute(slab, ("gx", "gy"), pairs))
    return received


def exchange_z(low, high):
    from_above = lax.ppermute(low, GZ, [((i + 1) % 8, i) for i in range(8)])
    from_below = lax.ppermute(high, GZ, [(i, (i + 1) % 8) for i in range(8)])
    return from_above, from_below


def add_up(part):
    for axis in ("gz_1", "gx", "gy", "gz_0"):
        size = lax.axis_size(axis)
        got = [lax.ppermute(part, axis, [(i, i ^ d) for i in range(size)]) for d in range(1, size)]
        part = part + got[0] if size == 2 else (part + got[0]) + (got[1] + got[2])
    return part


def body(residual_in, reaction, transport, congestion):
    given = (residual_in.reshape(8, N, N, LANES), reaction, transport, congestion)
    given = [pltpu.with_memory_space_constraint(g, pltpu.HBM) for g in given]
    core, half, packed = (8, N, N, LANES), (4, N, N, LANES), (E, LANES)
    scratch = [vmem((8, E, E, LANES)), vmem((8, E, E + 2 * PAD, LANES)), vmem((2, 8) + packed)]
    scratch += [vmem((2, 8, E + 2 * PAD, LANES))]
    scratch += [vmem((8, E, E, LANES)), vmem((8,) + packed)]
    shape = lambda *s: jax.ShapeDtypeStruct(s, F32)

    def surround(slabs, held):
        fields = sum(h.shape[0] for h in held)
        received = exchange(slabs)
        inside = call(core_kernel, [vmem((fields, E, E, LANES))] + [vmem((fields, N, LANES))] * 2, *held)
        wide, low, high = call(
            widen_kernel,
            [vmem((fields, E, E, LANES)), shape(fields, *packed), shape(fields, *packed)],
            *inside, *received, alias={0: 0},
        )
        return wide, *exchange_z(low, high)

    *slabs, res, rea, tra, con = call(
        pack_kernel,
        [shape(*slab_shape(20, w)) for w in WAYS] + [vmem(core)] + [vmem(half)] * 3,
        *given, far=True, scratch=[pltpu.SemaphoreType.DMA((4,))],
    )
    select, = call(weights_kernel, [pltpu.VMEM((E, 2 * LANES, 2 * LANES), jnp.bfloat16)])
    fields, upper, lower = surround(slabs, (res, rea, tra, con))
    inv, ginv, gcoefs, *made = call(
        first_kernel,
        [vmem((4, E, E, LANES)), vmem((2, 4) + packed), vmem((2, 8) + packed)] + [vmem(core)] * DEPTH,
        fields, upper, lower, select, scratch=scratch,
    )
    slabs = call(slab_kernel, [shape(*slab_shape(8, w)) for w in WAYS], made[-1])
    early, = call(early_gram_kernel, [vmem((EARLY + 1, LANES))], res, *made)
    wide, upper, lower = surround(slabs, made[-1:])
    more = call(second_kernel, [vmem(core)] * DEPTH, wide, upper, lower, select, inv, fields, ginv, gcoefs, scratch=scratch)
    basis = [res] + list(made) + list(more)
    part, = call(gram_kernel, [shape(ROWS, LANES)], early, *basis)
    gram = add_up(part)
    out, quality = call(update_kernel, [shape(*core), shape(1, 1)], gram, rea, tra, *basis[:ITERS])
    _, out = lax.while_loop(
        lambda state: jnp.logical_not(state[0] >= THIN),
        lambda state: (jnp.float32(1.0), careful(residual_in, reaction, transport, congestion)),
        (quality[0, 0], out.reshape(residual_in.shape)),
    )
    return out


def solution(mesh):
    torus = Mesh(
        mesh.devices.reshape(mesh.shape["gx"], mesh.shape["gy"], 4, 2), ("gx", "gy", "gz_0", "gz_1")
    )
    field = P(None, "gx", "gy", GZ)
    pair = P(None, None, "gx", "gy", GZ)
    return jax.shard_map(
        body, mesh=torus, in_specs=(pair, field, field, field), out_specs=pair, check_vma=False
    )
```

```python
import functools

import jax
import jax.numpy as jnp
from jax import lax
from jax.experimental import pallas as pl
from jax.experimental.pallas import tpu as pltpu
from jax.sharding import Mesh
from jax.sharding import PartitionSpec as P

ITERS = 8
LEVELS = 4
DEPTH = 4
N = 16
E = N + 2 * DEPTH
LANES = 128
PAD = 8
VECTORS = ITERS + 1
PAIRS = [(i, j) for j in range(VECTORS) for i in range(j + 1)]
EARLY = 15
ROWS = 48
GZ = ("gz_0", "gz_1")
GX_GY_GZ = ("gx", "gy", "gz_0", "gz_1")
THIN = 1e-3
SHIFT = (0.68, -0.68, 0.0, -0.392, 0.448, -0.57, 0.592, 0.208)
F32 = jnp.float32


def vmem(shape):
    return pltpu.VMEM(shape, F32)


def call(kernel, outs, *args, scratch=(), far=False, alias=None, cost=1000000):
    whole = pl.BlockSpec(memory_space=pltpu.VMEM)
    return pl.pallas_call(
        kernel,
        out_shape=outs,
        in_specs=[pl.BlockSpec(memory_space=pltpu.HBM) if far else whole] * len(args),
        out_specs=[pl.BlockSpec(memory_space=pltpu.SMEM) if out.shape == (1, 1) else whole for out in outs],
        scratch_shapes=list(scratch),
        input_output_aliases=alias or {},
        compiler_params=pltpu.CompilerParams(vmem_limit_bytes=LIMIT),
        cost_estimate=pl.CostEstimate(flops=cost, bytes_accessed=cost, transcendentals=0),
    )(*args)


LIMIT = 24 * 1024 * 1024
SLAB = {
    (-1, 0): (slice(0, DEPTH), slice(0, N)),
    (1, 0): (slice(N - DEPTH, N), slice(0, N)),
    (0, -1): (slice(0, N), slice(0, DEPTH)),
    (0, 1): (slice(0, N), slice(N - DEPTH, N)),
}
CORNERS = [(-1, -1), (1, 1), (-1, 1), (1, -1)]
STEPS_OUT = [(a, b) for a in range(1, DEPTH) for b in range(1, DEPTH) if a + b <= DEPTH]
WAYS = list(SLAB) + CORNERS


def landing(way):
    low = lambda d: DEPTH if d == 0 else (0 if d > 0 else DEPTH + N)
    size = lambda d: N if d == 0 else DEPTH
    return tuple(slice(low(d), low(d) + size(d)) for d in way)


def slab_shape(fields, way):
    if way in CORNERS:
        return (fields, len(STEPS_OUT), LANES)
    return (fields,) + tuple(N if d == 0 else DEPTH for d in way) + (LANES,)


def cut(core, f, outs, to):
    for out, way in zip(outs, WAYS):
        if way in SLAB:
            xs, ys = SLAB[way]
            out[to, :, :, :] = core[f, xs, ys, :]
        else:
            for n, (a, b) in enumerate(STEPS_OUT):
                x, y = (N - c if d > 0 else c - 1 for c, d in zip((a, b), way))
                out[to, n : n + 1, :] = core[f, x, y : y + 1, :]


def fill(wide, f, slabs):
    for slab, way in zip(slabs, WAYS):
        if way in SLAB:
            xs, ys = landing(way)
            wide[f, xs, ys, :] = slab[f]
        else:
            for n, (a, b) in enumerate(STEPS_OUT):
                x, y = (DEPTH - c if d > 0 else DEPTH + N + c - 1 for c, d in zip((a, b), way))
                wide[f, x, y : y + 1, :] = slab[f, n : n + 1, :]


def pack_kernel(res, rea, tra, con, *refs):
    slabs, held, done = refs[:8], refs[8:12], refs[12]
    copies = [pltpu.make_async_copy(src, dst, done.at[n]) for n, (src, dst) in enumerate(zip((res, rea, tra, con), held))]
    for copy in copies:
        copy.start()
    for copy, source, base in zip(copies, held, (0, 8, 12, 16)):
        copy.wait()

        @pl.loop(0, source.shape[0])
        def _(f):
            cut(source, f, slabs, base + f)


def slab_kernel(core, *outs):
    @pl.loop(0, 8)
    def _(f):
        cut(core, f, outs, f)


def pack_rows(rows, shape):
    slot = lax.broadcasted_iota(jnp.int32, shape, 1) // DEPTH
    lo = hi = jnp.zeros(shape, F32)
    for x, value in rows:
        rolled = pltpu.roll(value, DEPTH * x, 1) if x else value
        lo = jnp.where(slot == x, rolled, lo)
        hi = jnp.where(slot == (x - 1) % (LANES // DEPTH), rolled, hi)
    return lo, pltpu.roll(hi, DEPTH, 1)


def core_kernel(*refs):
    cores, (wide, low, high) = refs[:-3], refs[-3:]
    base = 0
    for core in cores:
        count = core.shape[0]

        @pl.loop(0, count)
        def _(f):
            for side in (0, DEPTH + N):
                wide[base + f, side : side + DEPTH] = jnp.zeros((DEPTH, E, LANES), F32)
            wide[base + f, DEPTH : DEPTH + N, DEPTH : DEPTH + N, :] = core[f]
            low[base + f], high[base + f] = pack_rows([(x + DEPTH, core[f, x]) for x in range(N)], (N, LANES))

        base = base + count


def widen_kernel(given, core_low, core_high, *refs):
    slabs, (wide, low, high) = refs[:8], refs[8:]
    slot = lax.broadcasted_iota(jnp.int32, (8, LANES), 1) // DEPTH
    row = lax.broadcasted_iota(jnp.int32, (8, LANES), 0)
    middle = (slot >= DEPTH) & (slot < DEPTH + N)
    tall = lax.broadcasted_iota(jnp.int32, (N, LANES), 1) // DEPTH
    tall = (tall >= DEPTH) & (tall < DEPTH + N)

    def widen(f):
        fill(wide, f, slabs)
        outside = [x for x in range(E) if not DEPTH <= x < DEPTH + N]
        sides = pack_rows([(x, wide[f, x]) for x in outside], (E, LANES))
        beyond = [
            (x, jnp.where(row < DEPTH, wide[f, x, 0:8, :], wide[f, x, E - 8 : E, :]))
            for x in range(DEPTH, DEPTH + N)
        ]
        ends = pack_rows(beyond, (8, LANES))
        for out, side, end, core in zip((low, high), sides, ends, (core_low, core_high)):
            out[f, 0:8, :] = jnp.where(middle & (row < DEPTH), end, side[0:8])
            out[f, 8 : E - 8, :] = side[8 : E - 8]
            out[f, E - 8 : E, :] = jnp.where(middle & (row >= 8 - DEPTH), end, side[E - 8 : E])
            span = slice(DEPTH, DEPTH + N)
            out[f, span, :] = jnp.where(tall, core[f], side[span])

    @pl.loop(0, wide.shape[0] // 4)
    def _(n):
        for m in range(4):
            widen(4 * n + m)


def weights_kernel(out):
    i = lax.broadcasted_iota(jnp.int32, (2 * LANES, 2 * LANES), 0)
    j = lax.broadcasted_iota(jnp.int32, (2 * LANES, 2 * LANES), 1)
    inside = (i < LANES) & (j < LANES) & ((i - j == 1) | (j - i == 1))

    @pl.loop(0, E)
    def _(x):
        slot = LANES + DEPTH * x
        above = ((i == LANES - 1) & (j == slot)) | ((i == slot) & (j == LANES - 1))
        below = ((i == 0) & (j == slot + 1)) | ((i == slot + 1) & (j == 0))
        out[x] = (inside | above | below).astype(F32).astype(jnp.bfloat16)


def halves(value):
    parts = []
    for _ in range(2):
        part = value.astype(jnp.bfloat16)
        parts.append(part)
        value = value - part.astype(F32)
    return parts


def steps(shifts, wide, ghosts, inv, coefs, ginv, gcoefs, select, wm, sm, gw, gs, along_z, ends, outs):
    lane = lax.broadcasted_iota(jnp.int32, (E, LANES), 1)
    place = lane % DEPTH
    wider = lax.broadcasted_iota(jnp.int32, (8 * E, LANES), 1)
    none = jnp.zeros((1, LANES), F32)

    @pl.loop(0, 8)
    def _(f):
        for x in range(E):
            sm[f, x, PAD - 1 : PAD, :] = none
            sm[f, x, PAD + E : PAD + E + 1, :] = none
        for side in range(2):
            gs[side, f, PAD - 1 : PAD, :] = none
            gs[side, f, PAD + E : PAD + E + 1, :] = none

    def precondition(w, v, transport, store):
        p = [None] * LEVELS
        carry = None
        for t in range(LEVELS - 1, -1, -1):
            top = w(t)
            carry = (top if carry is None else top + carry) * v(t)
            p[t] = carry
            store(t, carry)
        carry = None
        for t in range(LEVELS):
            top = w(LEVELS + t) + (6.0 * transport(t)) * p[t]
            carry = (top if carry is None else top + carry) * v(t)
            store(LEVELS + t, carry)

    middle = slice(PAD, PAD + E)
    for k, shift in enumerate(shifts):
        source = wide if k == 0 else wm
        beyond = [ghosts[side] if k == 0 else gw.at[side] for side in range(2)]
        final = k == len(shifts) - 1

        @pl.loop(k, E - k, unroll=2)
        def _(x):
            def store(f, value):
                sm[f, x, middle, :] = value

            precondition(lambda f: source[f, x], lambda t: inv[t, x], lambda t: coefs[t, x], store)

        for side in range(2):
            def store(f, value):
                gs[side, f, middle, :] = value

            precondition(lambda f: beyond[side][f], lambda t: ginv[side, t], lambda t: gcoefs[side, t], store)

        y0, rows = (DEPTH, N) if final else (0, E)
        span = slice(y0, y0 + rows)
        here = slice(PAD + y0, PAD + y0 + rows)
        upper, lower = (gs[side, :, here, :].reshape(8 * rows, LANES) for side in range(2))
        over = jnp.where(wider[: 8 * rows] % DEPTH == 1, pltpu.roll(lower, LANES - 2, 1), upper)
        outer = jnp.concatenate(halves(over), axis=0)
        packed = None
        for x in range(k + 1, E - k - 1):
            parts = halves(sm[:, x, here, :].reshape(8 * rows, LANES))
            both = jnp.concatenate([jnp.concatenate(parts, axis=0), outer], axis=1)
            matrix = select[x, :, :LANES] if final else select[x]
            moved = jnp.dot(both, matrix, preferred_element_type=F32)
            total = moved[: 8 * rows] + moved[8 * rows :]
            along_z[:, x, :rows, :] = total[:, :LANES].reshape(8, rows, LANES)
            if not final:
                packed = total[:, LANES:] if packed is None else packed + total[:, LANES:]
        if not final:
            ends[...] = packed.reshape(8, E, LANES)

        def beside_ghost(f):
            inner = ends[f]
            sums = []
            for side in range(2):
                value = gs[side, f, middle, :]
                before, after = pltpu.roll(value, 1, 1), pltpu.roll(value, LANES - 1, 1)
                if side == 0:
                    before = jnp.where(place == 0, inner, before)
                else:
                    after = jnp.where(place == DEPTH - 1, pltpu.roll(inner, 2, 1), after)
                total = before + after + gs[side, f, PAD - 1 : PAD + E - 1, :] + gs[side, f, PAD + 1 : PAD + E + 1, :]
                sums.append(total + pltpu.roll(value, DEPTH, 1) + pltpu.roll(value, LANES - DEPTH, 1))
            return sums

        if not final:
            for t in range(LEVELS):
                p_sums, r_sums = beside_ghost(t), beside_ghost(LEVELS + t)
                for side in range(2):
                    first = p_sums[side] + gcoefs[side, LEVELS + t] * gs[side, LEVELS + t, middle, :]
                    second = r_sums[side] - gcoefs[side, t] * p_sums[side]
                    if shift:
                        first = first + shift * beyond[side][t]
                        second = second + shift * beyond[side][LEVELS + t]
                    gw[side, t] = first
                    gw[side, LEVELS + t] = second

        @pl.loop(k + 1, E - k - 1, unroll=2)
        def _(x):
            def around(f):
                across = sm[f, x - 1, PAD + y0 : PAD + y0 + rows, :] + sm[f, x + 1, PAD + y0 : PAD + y0 + rows, :]
                along = sm[f, x, PAD + y0 - 1 : PAD + y0 + rows - 1, :] + sm[f, x, PAD + y0 + 1 : PAD + y0 + rows + 1, :]
                return along_z[f, x, :rows, :] + (across + along)

            for t in range(LEVELS):
                sp, sr = around(t), around(LEVELS + t)
                r = sm[LEVELS + t, x, PAD + y0 : PAD + y0 + rows, :]
                first = sp + coefs[LEVELS + t, x, span, :] * r
                second = sr - coefs[t, x, span, :] * sp
                if shift:
                    first = first + shift * source[t, x, span, :]
                    second = second + shift * source[LEVELS + t, x, span, :]
                if final:
                    outs[k][t, x - DEPTH] = first
                    outs[k][LEVELS + t, x - DEPTH] = second
                else:
                    wm[t, x] = first
                    wm[LEVELS + t, x] = second

        if not final:
            @pl.loop(0, N)
            def _(x):
                for f in range(8):
                    outs[k][f, x] = wm[f, x + DEPTH, DEPTH : DEPTH + N, :]


def first_kernel(wide, upper, lower, select, inv, ginv, gcoefs, *refs):
    outs, scratch = refs[:DEPTH], refs[DEPTH:]
    place = [lax.axis_index("gx"), lax.axis_index("gy"), lax.axis_index(GZ)]
    lane = lax.broadcasted_iota(jnp.int32, (E, LANES), 1)
    row = lax.broadcasted_iota(jnp.int32, (E, LANES), 0)
    slot = lane // DEPTH

    def within(index, spot):
        return (index < E) & ((spot > 0) | (index >= DEPTH)) & ((spot < 3) | (index < DEPTH + N))

    y_in = within(row, place[1])
    ym = y_in.astype(F32)
    xy = (y_in & within(slot, place[0])).astype(F32)
    ends = ((place[2] < 7).astype(F32), (place[2] > 0).astype(F32))

    @pl.loop(0, E)
    def _(x):
        mask = ym * within(x, place[0]).astype(F32)
        for t in range(LEVELS):
            inv[t, x] = mask / (7.0 + wide[8 + t, x])

    for side, ghost in enumerate((upper, lower)):
        for t in range(LEVELS):
            ginv[side, t] = (xy * ends[side]) / (7.0 + ghost[8 + t])
            gcoefs[side, t] = ghost[12 + t]
            gcoefs[side, LEVELS + t] = ghost[16 + t]

    steps(SHIFT[:DEPTH], wide, (upper, lower), inv, wide.at[12:20], ginv, gcoefs, select, *scratch, outs)


def second_kernel(wide, upper, lower, select, inv, coefs, ginv, gcoefs, *refs):
    outs, scratch = refs[:DEPTH], refs[DEPTH:]
    steps(SHIFT[DEPTH:], wide, (upper, lower), inv, coefs.at[12:20], ginv, gcoefs, select, *scratch, outs)


def products(vectors, pairs):
    used = sorted({v for pair in pairs for v in pair})

    def add(i, sums):
        held = {v: vectors[v][i // N, i % N] for v in used}
        new = []
        for (a, b), total in zip(pairs, sums):
            product = held[a] * held[b]
            new.append(total + (product[:8] + product[8:]))
        return tuple(new)

    sums = lax.fori_loop(0, 8 * N, add, tuple(jnp.zeros((8, LANES), F32) for _ in pairs), unroll=4)
    return [jnp.sum(total, axis=0, keepdims=True) for total in sums]


def early_gram_kernel(*refs):
    vectors, out = refs[:-1], refs[-1]
    for n, row in enumerate(products(vectors, PAIRS[:EARLY])):
        out[n : n + 1, :] = row
    out[EARLY:, :] = jnp.zeros((1, LANES), F32)


def gram_kernel(early, *refs):
    vectors, out, rows = refs[:-2], refs[-2], refs[-1]
    rows[:EARLY, :] = early[:EARLY, :]
    for n, row in enumerate(products(vectors, PAIRS[EARLY:])):
        rows[EARLY + n : EARLY + n + 1, :] = row
    rows[len(PAIRS) :, :] = jnp.zeros((ROWS - len(PAIRS), LANES), F32)
    spread = jnp.where(on_diagonal(), jnp.sum(rows[...], axis=1, keepdims=True), 0.0)
    out[...] = jnp.broadcast_to(jnp.sum(spread, axis=0, keepdims=True), (8, LANES))


def on_diagonal():
    row = lax.broadcasted_iota(jnp.int32, (ROWS, LANES), 0)
    return row == lax.broadcasted_iota(jnp.int32, (ROWS, LANES), 1)


def solve(gram):
    entry = {pair: gram[n : n + 1] for n, pair in enumerate(PAIRS)}
    upper = {}
    least = jnp.ones_like(entry[0, 0])
    for i in range(VECTORS):
        pivot = entry[i, i]
        for m in range(i):
            pivot = pivot - upper[m, i] * upper[m, i]
        least = jnp.minimum(least, pivot / entry[i, i])
        pivot = jnp.maximum(pivot, 1e-7 * entry[i, i])
        root = jnp.sqrt(pivot)
        upper[i, i] = root
        for j in range(i + 1, VECTORS):
            value = entry[i, j]
            for m in range(i):
                value = value - upper[m, i] * upper[m, j]
            upper[i, j] = value / root
    columns = []
    for c in range(ITERS):
        column = [(1.0 + SHIFT[c]) * upper[i, c] - upper[i, c + 1] for i in range(c + 1)]
        columns.append(column + [-upper[c + 1, c + 1]])
    return least, least_squares(columns, upper[0, 0], ITERS)


def least_squares(columns, beta, steps):
    rotations = []
    target = [beta] + [jnp.zeros_like(beta)] * steps
    upper = []
    for column_index in range(steps):
        column = list(columns[column_index])
        for place, (cosine, sine) in enumerate(rotations):
            upper_entry = cosine * column[place] + sine * column[place + 1]
            lower_entry = -sine * column[place] + cosine * column[place + 1]
            column[place], column[place + 1] = (upper_entry, lower_entry)
        radius = jnp.sqrt(column[column_index] ** 2 + column[column_index + 1] ** 2)
        cosine = column[column_index] / radius
        sine = column[column_index + 1] / radius
        column[column_index] = radius
        rotations.append((cosine, sine))
        target[column_index], target[column_index + 1] = (
            cosine * target[column_index],
            -sine * target[column_index],
        )
        upper.append(column[: column_index + 1])
    solved = [None] * steps
    for row_index in range(steps - 1, -1, -1):
        accum = target[row_index]
        for later_index in range(row_index + 1, steps):
            accum = accum - upper[later_index][row_index] * solved[later_index]
        solved[row_index] = accum / upper[row_index][row_index]
    return solved


def with_halo(shard, sides, width):
    edges = {}
    for axis, dim in sides:
        size, length = (lax.axis_size(axis), shard.shape[dim])
        up = [(i, (i + 1) % size) for i in range(size - 1)]
        last = lax.slice_in_dim(shard, length - width, length, axis=dim)
        first = lax.slice_in_dim(shard, 0, width, axis=dim)
        edges[dim] = (
            lax.ppermute(last, axis, up),
            lax.ppermute(first, axis, [(b, a) for a, b in up]),
        )
    done = []
    for _, dim in sides:
        low, high = edges[dim]
        around = [(width, width) if d in done else (0, 0) for d in range(shard.ndim)]
        shard = jnp.concatenate([jnp.pad(low, around), shard, jnp.pad(high, around)], axis=dim)
        done.append(dim)
    return shard


def stencil(padded):
    center = padded[..., 1:-1, 1:-1, 1:-1]
    beside = padded[..., 2:, 1:-1, 1:-1] + padded[..., :-2, 1:-1, 1:-1]
    beside = beside + padded[..., 1:-1, 2:, 1:-1] + padded[..., 1:-1, :-2, 1:-1]
    beside = beside + padded[..., 1:-1, 1:-1, 2:] + padded[..., 1:-1, 1:-1, :-2]
    return 6.0 * center - beside


def jacobian(vector, lapped, reaction, transport, congestion):
    value_part, density_part = (vector[0], vector[1])
    later = jnp.concatenate([value_part[1:], jnp.zeros_like(value_part[:1])], 0)
    earlier = jnp.concatenate([jnp.zeros_like(density_part[:1]), density_part[:-1]], 0)
    first = (
        (value_part - later)
        + lapped[0]
        + reaction * value_part
        - congestion * density_part
    )
    second = (
        (density_part - earlier)
        + lapped[1]
        + reaction * density_part
        - transport * lapped[0]
    )
    return jnp.stack([first, second], 0)


def precondition(vector, reaction, transport):
    levels = vector.shape[1]
    diag = 7.0 + reaction
    value_levels = [None] * levels
    carry = jnp.zeros_like(vector[0, 0])
    for level in range(levels - 1, -1, -1):
        carry = (vector[0, level] + carry) / diag[level]
        value_levels[level] = carry
    density_levels = []
    carry = jnp.zeros_like(vector[1, 0])
    for level in range(levels):
        carry = (
            vector[1, level] + carry + 6.0 * transport[level] * value_levels[level]
        ) / diag[level]
        density_levels.append(carry)
    return jnp.stack([jnp.stack(value_levels, 0), jnp.stack(density_levels, 0)], 0)


def lapped_field(search):
    padded = with_halo(search, (("gx", 2), ("gy", 3), (GZ, 4)), 1)
    return stencil(padded)


def careful(residual_in, reaction, transport, congestion):
    whole = lambda part: functools.reduce(lax.psum, GX_GY_GZ, part)
    spread = (slice(None),) + (None,) * residual_in.ndim
    beta = jnp.sqrt(whole(jnp.sum(residual_in * residual_in)))
    basis = jnp.zeros((VECTORS,) + residual_in.shape, F32).at[0].set(residual_in / beta)

    def column(c, state):
        basis, h = state
        search = precondition(lax.dynamic_index_in_dim(basis, c, 0, False), reaction, transport)
        image = jacobian(search, lapped_field(search), reaction, transport, congestion)
        coeffs = whole(jnp.sum(basis * image, axis=tuple(range(1, basis.ndim))))
        image = image - jnp.sum(coeffs[spread] * basis, axis=0)
        height = jnp.sqrt(whole(jnp.sum(image * image)))
        basis = lax.dynamic_update_index_in_dim(basis, image / height, c + 1, 0)
        coeffs = jnp.where(jnp.arange(VECTORS) == c + 1, height, coeffs)
        return basis, lax.dynamic_update_index_in_dim(h, coeffs, c, 0)

    basis, h = lax.fori_loop(0, ITERS, column, (basis, jnp.zeros((ITERS, VECTORS), F32)))
    columns = [[h[c, i] for i in range(c + 2)] for c in range(ITERS)]
    weights = jnp.stack(least_squares(columns, beta, ITERS))
    return precondition(jnp.sum(weights[spread] * basis[:ITERS], axis=0), reaction, transport)


def update_kernel(gram, rea, tra, *refs):
    vectors, (out, quality) = refs[:ITERS], refs[ITERS:]
    spread = jnp.where(on_diagonal(), gram[0:1, :], 0.0)
    whole = jnp.broadcast_to(jnp.sum(spread, axis=1, keepdims=True), (ROWS, LANES))
    least, rows = solve(whole)
    quality[0, 0] = least[0, 0]
    weights = [jnp.broadcast_to(row, (N, LANES)) for row in rows]

    @pl.loop(0, N, unroll=2)
    def _(x):
        def mixed(f):
            total = weights[0] * vectors[0][f, x]
            for weight, vector in zip(weights[1:], vectors[1:]):
                total = total + weight * vector[f, x]
            return total

        inverse = [1.0 / (7.0 + rea[t, x]) for t in range(LEVELS)]
        p = [None] * LEVELS
        carry = None
        for t in range(LEVELS - 1, -1, -1):
            top = mixed(t)
            carry = (top if carry is None else top + carry) * inverse[t]
            p[t] = carry
            out[t, x] = carry
        carry = None
        for t in range(LEVELS):
            top = mixed(LEVELS + t) + 6.0 * tra[t, x] * p[t]
            carry = (top if carry is None else top + carry) * inverse[t]
            out[LEVELS + t, x] = carry


def exchange(slabs):
    received = []
    for slab, (dx, dy) in zip(slabs, WAYS):
        pairs = [(x * 4 + y, (x + dx) % 4 * 4 + (y + dy) % 4) for x in range(4) for y in range(4)]
        received.append(lax.ppermute(slab, ("gx", "gy"), pairs))
    return received


def exchange_z(low, high):
    from_above = lax.ppermute(low, GZ, [((i + 1) % 8, i) for i in range(8)])
    from_below = lax.ppermute(high, GZ, [(i, (i + 1) % 8) for i in range(8)])
    return from_above, from_below


def add_up(part):
    for axis in ("gz_1", "gx", "gy", "gz_0"):
        size = lax.axis_size(axis)
        got = [lax.ppermute(part, axis, [(i, i ^ d) for i in range(size)]) for d in range(1, size)]
        part = part + got[0] if size == 2 else (part + got[0]) + (got[1] + got[2])
    return part


def body(residual_in, reaction, transport, congestion):
    given = (residual_in.reshape(8, N, N, LANES), reaction, transport, congestion)
    given = [pltpu.with_memory_space_constraint(g, pltpu.HBM) for g in given]
    core, half, packed = (8, N, N, LANES), (4, N, N, LANES), (E, LANES)
    scratch = [vmem((8, E, E, LANES)), vmem((8, E, E + 2 * PAD, LANES)), vmem((2, 8) + packed)]
    scratch += [vmem((2, 8, E + 2 * PAD, LANES))]
    scratch += [vmem((8, E, E, LANES)), vmem((8,) + packed)]
    shape = lambda *s: jax.ShapeDtypeStruct(s, F32)

    def surround(slabs, held):
        fields = sum(h.shape[0] for h in held)
        received = exchange(slabs)
        inside = call(core_kernel, [vmem((fields, E, E, LANES))] + [vmem((fields, N, LANES))] * 2, *held)
        wide, low, high = call(
            widen_kernel,
            [vmem((fields, E, E, LANES)), shape(fields, *packed), shape(fields, *packed)],
            *inside, *received, alias={0: 0},
        )
        return wide, *exchange_z(low, high)

    *slabs, res, rea, tra, con = call(
        pack_kernel,
        [shape(*slab_shape(20, w)) for w in WAYS] + [vmem(core)] + [vmem(half)] * 3,
        *given, far=True, scratch=[pltpu.SemaphoreType.DMA((4,))],
    )
    select, = call(weights_kernel, [pltpu.VMEM((E, 2 * LANES, 2 * LANES), jnp.bfloat16)])
    fields, upper, lower = surround(slabs, (res, rea, tra, con))
    inv, ginv, gcoefs, *made = call(
        first_kernel,
        [vmem((4, E, E, LANES)), vmem((2, 4) + packed), vmem((2, 8) + packed)] + [vmem(core)] * DEPTH,
        fields, upper, lower, select, scratch=scratch,
    )
    slabs = call(slab_kernel, [shape(*slab_shape(8, w)) for w in WAYS], made[-1])
    early, = call(early_gram_kernel, [vmem((EARLY + 1, LANES))], res, *made)
    wide, upper, lower = surround(slabs, made[-1:])
    more = call(second_kernel, [vmem(core)] * DEPTH, wide, upper, lower, select, inv, fields, ginv, gcoefs, scratch=scratch)
    basis = [res] + list(made) + list(more)
    part, = call(gram_kernel, [shape(8, LANES)], early, *basis, scratch=[vmem((ROWS, LANES))])
    gram = add_up(part)
    out, quality = call(update_kernel, [shape(*core), shape(1, 1)], gram, rea, tra, *basis[:ITERS])
    _, out = lax.while_loop(
        lambda state: jnp.logical_not(state[0] >= THIN),
        lambda state: (jnp.float32(1.0), careful(residual_in, reaction, transport, congestion)),
        (quality[0, 0], out.reshape(residual_in.shape)),
    )
    return out


def solution(mesh):
    torus = Mesh(
        mesh.devices.reshape(mesh.shape["gx"], mesh.shape["gy"], 4, 2), ("gx", "gy", "gz_0", "gz_1")
    )
    field = P(None, "gx", "gy", GZ)
    pair = P(None, None, "gx", "gy", GZ)
    return jax.shard_map(
        body, mesh=torus, in_specs=(pair, field, field, field), out_specs=pair, check_vma=False
    )
```
